32 devices in a mesh: head: 2 (over core), blk: 16 (over z, y, x).
Axes of the slice: x: 2, y: 2, z: 4, core: 2. Of those that a mesh axis runs over, the one named last changes fastest.
Arguments:
- tokens: bfloat16 [4096, 1536], P(('head', 'blk')), may hold values from -6 to 6
- lengths: int32 [12], replicated, may hold values from 1 to 2048, 4096 in all
- expert_ids: int32 [4096, 2], P(('head', 'blk')), may hold values from 0 to 15, all different within a row; in each aligned block of 128 rows (0 to 127, 128 to 255, ...) at most 48 rows name the same one
- w_query: bfloat16 [1536, 1536], P(('head', 'blk')), may hold values from -0.15625 to 0.15625
- w_key: bfloat16 [1536, 512], P(('head', 'blk')), may hold values from -0.15625 to 0.15625
- w_value: bfloat16 [1536, 512], P(('head', 'blk')), may hold values from -0.15625 to 0.15625
- w_out: bfloat16 [1536, 1536], P(('head', 'blk')), may hold values from -2.5 to 2.5
- w_router: bfloat16 [1536, 16], P(('head', 'blk')), may hold values from -0.15625 to 0.15625
- gain_attn: bfloat16 [1536], P(('head', 'blk')), may hold values from 0.5 to 1.5
- gain_moe: bfloat16 [1536], P(('head', 'blk')), may hold values from 0.5 to 1.5
- w_gate: bfloat16 [16, 1536, 1024], P('blk', None, 'head'), may hold values from -0.15625 to 0.15625
- w_up: bfloat16 [16, 1536, 1024], P('blk', None, 'head'), may hold values from -0.15625 to 0.15625
- w_down: bfloat16 [16, 1024, 1536], P('blk', 'head'), may hold values from -0.1875 to 0.1875
- cotangent: bfloat16 [4096, 1536], P(('head', 'blk')), may hold values from -6 to 6
Outputs:
- output: bfloat16 [4096, 1536], P(('head', 'blk'))
- input_grad: bfloat16 [4096, 1536], P(('head', 'blk'))
- grad_query: float32 [1536, 1536], P(('head', 'blk'))
- grad_key: float32 [1536, 512], P(('head', 'blk'))
- grad_value: float32 [1536, 512], P(('head', 'blk'))
- grad_out: float32 [1536, 1536], P(('head', 'blk'))
- grad_router: float32 [1536, 16], P(('head', 'blk'))
- grad_gain_attn: float32 [1536], P(('head', 'blk'))
- grad_gain_moe: float32 [1536], P(('head', 'blk'))
- grad_gate: float32 [16, 1536, 1024], P('blk', None, 'head')
- grad_up: float32 [16, 1536, 1024], P('blk', None, 'head')
- grad_down: float32 [16, 1024, 1536], P('blk', 'head')
The draws below stay inside these ranges and needn't reach their ends.
Inputs may be any that keep to these rules, and one draw needn't show every extreme that they name: The last entry counts the padding tokens at the end of the token order; the others are the documents' lengths in order; all entries add up to 4096. `expert_ids`: each token names two different experts. Among the 128 tokens of one device no expert is named by more than 48 tokens, and some expert reaches that bound.
All inputs are finite; a program needn't handle non-finite values.
Results may differ from the reference program's by a relative error of at most 0.025.
Values may be sent and summed in bfloat16 or wider, within the bound.
No kernel may reach another device: no remote copies, remote signals or barrier semaphores. Data moves between devices by JAX's collectives and lax.ppermute only.
A program may use at most 256 MiB of HBM per device.

```python
import math
import jax
import jax.numpy as jnp
import numpy as np
from jax import lax

D = 1536
HQ = 24
HK = 8
HD = 64
FF = 1024
TOK_DEV = 128
NSEG = 12
TOKENS = 4096
EXPERTS = 16
CAP = 24
MOST = 2048
ROUTE_MOST = 48


def steps_of(own_key, dims, pieces, least, high):
    def one(position, shards_of):
        heights = jax.random.uniform(jax.random.fold_in(jax.random.fold_in(own_key, 6), position), (shards_of,), jnp.float32, least / len(pieces), high / len(pieces))
        return jnp.repeat(jnp.exp(heights), dims[position] // shards_of).reshape((-1,) + (1,) * (len(dims) - position - 1))

    factor_of = one(*pieces[0])
    for cut in pieces[1:]:
        factor_of = factor_of * one(*cut)
    return factor_of


def length_profile(amount, total, limit, skew):
    loads = [(1 << 20) // math.isqrt(standing ** skew) + 1 for standing in range(2, amount + 1)]
    rest, given = total - limit - (amount - 1), [1] * (amount - 1)
    while rest > 0:
        free = [i for i in range(amount - 1) if given[i] < limit]
        whole, left = sum([loads[i] for i in free]), rest
        for i in free:
            extra = min(limit - given[i], max(1, left * loads[i] // whole), rest)
            given[i] = given[i] + extra
            rest = rest - extra
    return np.array([limit] + given)


def ragged(key, amount, total, reach, skew):
    if amount == 2:
        one = jax.random.randint(key, (), max(1, total - reach), min(reach, total - 1) + 1)
        return jnp.stack([one, total - one])
    sizes = jnp.asarray(length_profile(amount, total, reach, skew), jnp.int32)
    couples = (amount - 1) // 2
    giver, sink = sizes[1:1 + 2 * couples:2], sizes[2:2 + 2 * couples:2]
    margin = jnp.minimum(giver - 1, reach - sink)
    passed = jax.random.randint(jax.random.fold_in(key, 1), (couples,), 0, 1 << 20) % (margin + 1)
    sizes = sizes.at[1:1 + 2 * couples:2].set(giver - passed).at[2:2 + 2 * couples:2].set(sink + passed)
    return sizes[jax.random.permutation(jax.random.fold_in(key, 2), amount)]


def shared_out(own_key, own, number, rows, amount, top, limit, slope):
    sequence = jax.random.permutation(own_key, amount)
    crowded, common = shares(amount, rows * top, limit, slope, True), shares(amount, rows * top, limit, slope, False)
    places = jnp.arange(amount)

    def named(tallies, offset_by):
        used = int((tallies > 0).sum())
        fixed = max(1, used // 4)
        moved = fixed + (places - fixed + offset_by * (used - fixed)) % max(1, amount - fixed)
        return jnp.zeros((amount,), jnp.int32).at[sequence[jnp.where(places < fixed, places, moved)]].set(jnp.asarray(tallies, jnp.int32))

    tallies = jnp.where(number % 4 == 0, named(crowded, number // 4), named(common, number - number // 4 - 1))
    mixed = jax.random.permutation(jax.random.fold_in(own, 3), amount)
    source_of, taker = mixed[0:amount // 2 * 2:2], mixed[1:amount // 2 * 2:2]
    room = jnp.minimum(tallies[source_of] - 1, limit - tallies[taker]) // 2
    room = jnp.where((source_of == sequence[0]) | (taker == sequence[0]) | (tallies[taker] == 0), 0, jnp.maximum(room, 0))
    moved = jax.random.randint(jax.random.fold_in(own, 4), (amount // 2,), 0, 1 << 20) % (room + 1)
    tallies = tallies.at[source_of].add(-moved).at[taker].add(moved)
    items = jnp.searchsorted(jnp.cumsum(tallies), jnp.arange(rows * top), side="right").astype(jnp.int32)
    listing = items.reshape(top, rows).T
    listing = listing[jax.random.permutation(jax.random.fold_in(own, 1), rows)]
    offset_by = jax.random.randint(jax.random.fold_in(own, 2), (rows, 1), 0, top)
    return jnp.take_along_axis(listing, (jnp.arange(top)[None, :] + offset_by) % top, axis=1)


def shares(amount, total, most, slope, full):
    weights = [(1 << 20) // math.isqrt(grade ** slope) + 1 for grade in range(1, amount + 1)]
    largest = most if full else min(most, max(-(-total // amount), total * weights[0] // sum(weights)))
    least = 1 if total - largest >= amount - 1 else 0
    counts, rest = [largest] + [least] * (amount - 1), total - largest - least * (amount - 1)
    while rest > 0:
        candidates = [i for i in range(1, amount) if counts[i] < largest] or [i for i in range(1, amount) if counts[i] < most]
        mass, left = sum([weights[i] for i in candidates]), rest
        for i in candidates:
            addition = min(most - counts[i], max(1, left * weights[i] // mass), rest)
            counts[i] = counts[i] + addition
            rest = rest - addition
    return np.array(counts)


def normal_values(stream_key, shape, spread, limit, pieces=(), kind=jnp.bfloat16):
    array = spread * jax.random.normal(stream_key, shape, jnp.float32)
    if pieces:
        array = array * steps_of(stream_key, shape, pieces, -0.22, 0.18)
    return jnp.clip(array, -limit, limit).astype(kind)


def setup_inputs(seed: int = 0) -> dict:
    seeds = jax.random.split(jax.random.key(seed), 15)
    tokens = normal_values(seeds[0], (TOKENS, D), 1.0, 6.0, ((0, 32),))
    lengths = ragged(seeds[1], NSEG, TOKENS, MOST, 1).astype(jnp.int32)
    expert_ids_keys = jax.random.split(jax.random.fold_in(seeds[2], 1), TOKENS // TOK_DEV)
    expert_ids_turns = jax.random.permutation(jax.random.fold_in(seeds[2], 3), TOKENS // TOK_DEV)
    expert_ids = jax.vmap(lambda own, number: shared_out(jax.random.fold_in(seeds[2], 2), own, number, TOK_DEV, EXPERTS, 2, ROUTE_MOST, 1))(expert_ids_keys, expert_ids_turns).reshape((TOKENS, 2))
    w_query = normal_values(seeds[3], (D, HQ * HD), D ** -0.5, 0.15625, ((0, 32),))
    w_key = normal_values(seeds[4], (D, HK * HD), D ** -0.5, 0.15625, ((0, 32),))
    w_value = normal_values(seeds[5], (D, HK * HD), D ** -0.5, 0.15625, ((0, 32),))
    w_out = normal_values(seeds[6], (HQ * HD, D), (max(1, HQ * HD // 256)) ** -0.5, 2.5, ((0, 32),))
    w_router = normal_values(seeds[7], (D, EXPERTS), D ** -0.5, 0.15625, ((0, 32),))
    gain_attn = jnp.clip(1.0 + 0.1 * jax.random.normal(seeds[8], (D,), jnp.float32), 0.5, 1.5).astype(jnp.bfloat16)
    gain_moe = jnp.clip(1.0 + 0.1 * jax.random.normal(seeds[9], (D,), jnp.float32), 0.5, 1.5).astype(jnp.bfloat16)
    w_gate = normal_values(seeds[10], (EXPERTS, D, FF), D ** -0.5, 0.15625, ((0, 16), (2, 2)))
    w_up = normal_values(seeds[11], (EXPERTS, D, FF), D ** -0.5, 0.15625, ((0, 16), (2, 2)))
    w_down = normal_values(seeds[12], (EXPERTS, FF, D), FF ** -0.5, 0.1875, ((0, 16), (1, 2)))
    cotangent = normal_values(seeds[13], (TOKENS, D), 1.0, 6.0, ((0, 32),))
    return dict(tokens=tokens, lengths=lengths, expert_ids=expert_ids, w_query=w_query, w_key=w_key, w_value=w_value, w_out=w_out, w_router=w_router, gain_attn=gain_attn, gain_moe=gain_moe, w_gate=w_gate, w_up=w_up, w_down=w_down, cotangent=cotangent)


EPS = 1e-05
NEG = -1e+30
HIGH = lax.Precision.HIGHEST

@jax.custom_vjp
def low(v):
    return lax.optimization_barrier(v.astype(jnp.bfloat16)).astype(jnp.float32)

@jax.custom_vjp
def low_back(v):
    return v

def low_keep(v):
    return (low(v), None)

def low_pass(kept, grad):
    return (grad,)

def back_keep(v):
    return (v, None)

def back_low(kept, grad):
    return (low(grad),)
low.defvjp(low_keep, low_pass)
low_back.defvjp(back_keep, back_low)

def product(left, right):
    return jnp.dot(left, right, precision=HIGH, preferred_element_type=jnp.float32)

def rms_scale(values):
    return lax.rsqrt(lax.optimization_barrier(jnp.mean(values * values, axis=-1, keepdims=True)) + EPS)

def reference(tokens, lengths, expert_ids, w_query, w_key, w_value, w_out, w_router, gain_attn, gain_moe, w_gate, w_up, w_down, cotangent):
    positions = jnp.arange(TOKENS, dtype=jnp.int32)
    seq_ends = jnp.cumsum(lengths).astype(jnp.int32)
    doc_ids = lax.optimization_barrier(jnp.sum((positions[:, None] >= seq_ends[None, :]).astype(jnp.int32), axis=1)).astype(jnp.int32)
    valid_bool = doc_ids < NSEG - 1
    valid_rows = valid_bool.astype(jnp.float32)[:, None]
    group = HQ // HK
    blocks = TOKENS // TOK_DEV
    pair_experts = expert_ids.reshape(blocks, 2 * TOK_DEV).astype(jnp.int32)
    live_pairs = jnp.repeat(valid_bool, 2).reshape(blocks, 2 * TOK_DEV)
    onehot = ((pair_experts[:, :, None] == jnp.arange(EXPERTS, dtype=jnp.int32)[None, None, :]) & live_pairs[:, :, None]).astype(jnp.int32)
    earlier = (jnp.cumsum(onehot, axis=1).astype(jnp.int32) - onehot).astype(jnp.int32)
    slot_index = lax.optimization_barrier(jnp.sum(earlier * onehot, axis=2)).astype(jnp.int32)
    kept_pairs = live_pairs & (slot_index < CAP)
    flat_index = (pair_experts * CAP + slot_index).astype(jnp.int32)
    slot_table = ((flat_index[:, None, :] == jnp.arange(EXPERTS * CAP, dtype=jnp.int32)[None, :, None]) & kept_pairs[:, None, :]).astype(jnp.float32)
    pick_table = (expert_ids[:, :, None] == jnp.arange(EXPERTS, dtype=jnp.int32)[None, None, :]).astype(jnp.float32)
    qblock = min(512, TOKENS)
    window = min(MOST + qblock, TOKENS)
    scale = HD ** (-0.5)

    def attention(query, key, value):

        def one_block(index):
            start = (index * qblock).astype(jnp.int32)
            key_start = jnp.maximum(start + qblock - window, 0).astype(jnp.int32)
            q_part = lax.dynamic_slice_in_dim(query, start, qblock, 0).reshape(qblock, HK, group, HD)
            k_part = lax.dynamic_slice_in_dim(key, key_start, window, 0)
            v_part = lax.dynamic_slice_in_dim(value, key_start, window, 0)
            q_doc = lax.dynamic_slice_in_dim(doc_ids, start, qblock, 0)
            k_doc = lax.dynamic_slice_in_dim(doc_ids, key_start, window, 0)
            q_pos = start + jnp.arange(qblock, dtype=jnp.int32)
            k_pos = key_start + jnp.arange(window, dtype=jnp.int32)
            allowed = (q_doc[:, None] == k_doc[None, :]) & (k_pos[None, :] <= q_pos[:, None])
            scores = jnp.einsum('qhgd,khd->hgqk', q_part, k_part, precision=HIGH) * scale
            scores = low_back(scores)
            scores = jnp.where(allowed[None, None, :, :], scores, NEG)
            probs = low(jax.nn.softmax(scores, axis=-1))
            mixed = jnp.einsum('hgqk,khd->qhgd', probs, v_part, precision=HIGH)
            return mixed.reshape(qblock, HQ * HD)
        parts = lax.map(jax.checkpoint(one_block), jnp.arange(TOKENS // qblock, dtype=jnp.int32))
        return parts.reshape(TOKENS, HQ * HD)

    def experts(normed_two, mix_weights, wg_f, wu_f, wd_f):
        pair_rows = jnp.repeat(normed_two, 2, axis=0).reshape(blocks, 2 * TOK_DEV, D)
        sent = low_back(jnp.einsum('gsj,gjd->gsd', slot_table, pair_rows, precision=HIGH))
        per_expert = sent.reshape(blocks, EXPERTS, CAP, D).transpose(1, 0, 2, 3).reshape(EXPERTS, blocks * CAP, D)

        def apply_expert(args):
            rows, gate_mat, up_mat, down_mat = args
            gate_pre = low_back(product(rows, gate_mat))
            up_pre = low_back(product(rows, up_mat))
            inner_act = low(jax.nn.silu(gate_pre) * up_pre)
            return low(low_back(product(inner_act, down_mat)))
        results = lax.map(jax.checkpoint(apply_expert), (per_expert, wg_f, wu_f, wd_f))
        returned = results.reshape(EXPERTS, blocks, CAP, D).transpose(1, 0, 2, 3).reshape(blocks, EXPERTS * CAP, D)
        y_pairs = jnp.einsum('gsj,gsd->gjd', slot_table, returned, precision=HIGH).reshape(TOKENS, 2, D)
        return lax.optimization_barrier(jnp.sum(mix_weights[:, :, None] * y_pairs, axis=1))

    def forward(x_float, wq_f, wk_f, wv_f, wo_f, wr_f, ga_f, gm_f, wg_f, wu_f, wd_f):
        normed_one = low(x_float * rms_scale(x_float) * ga_f)
        query = low(low_back(product(normed_one, wq_f))).reshape(TOKENS, HQ, HD)
        key = low(low_back(product(normed_one, wk_f))).reshape(TOKENS, HK, HD)
        value = low(low_back(product(normed_one, wv_f))).reshape(TOKENS, HK, HD)
        attn = low(low_back(attention(query, key, value)))
        hidden_one = x_float + low_back(product(attn, wo_f))
        normed_two = low(hidden_one * rms_scale(hidden_one) * gm_f)
        logits = low_back(product(normed_two, wr_f))
        chosen = lax.optimization_barrier(jnp.sum(pick_table * logits[:, None, :], axis=2))
        mix_weights = jax.nn.softmax(chosen, axis=1)
        moe_part = experts(normed_two, mix_weights, wg_f, wu_f, wd_f)
        return valid_rows * (hidden_one + moe_part)
    inputs = (tokens.astype(jnp.float32), w_query.astype(jnp.float32), w_key.astype(jnp.float32), w_value.astype(jnp.float32), w_out.astype(jnp.float32), w_router.astype(jnp.float32), gain_attn.astype(jnp.float32), gain_moe.astype(jnp.float32), w_gate.astype(jnp.float32), w_up.astype(jnp.float32), w_down.astype(jnp.float32))
    result, pullback = jax.vjp(forward, *inputs)
    grads = pullback(cotangent.astype(jnp.float32))
    return (result.astype(jnp.bfloat16), grads[0].astype(jnp.bfloat16), grads[1], grads[2], grads[3], grads[4], grads[5], grads[6], grads[7], grads[8], grads[9], grads[10])
```

```python
import functools

import jax
import jax.numpy as jnp
from jax import lax
from jax.experimental import pallas as pl
from jax.experimental.pallas import tpu as pltpu
from jax.sharding import Mesh
from jax.sharding import PartitionSpec as P

D = 1536
HQ = 24
HK = 8
HD = 64
GROUP = HQ // HK
QW = GROUP * HD
KV = 2 * HD
QKV = QW + KV
LANE = 128
EPS = 1e-05
NEG = -1e30
BQ = 256
F32 = jnp.float32
BF16 = jnp.bfloat16

PLANE = ("head", "hg")
BLK = ("tg", "hg")
ALL = ("head", "tg", "hg")


def pad_up(count):
    return -(-count // LANE) * LANE


def rms_scale(values):
    return lax.rsqrt(jnp.mean(values * values, axis=-1, keepdims=True) + EPS)


def doc_ranges(lengths_ref, segments, q_pos, first, key_rows):
    start = jnp.zeros_like(q_pos)
    low = jnp.int32(0)
    end = jnp.int32(0)
    for j in range(segments):
        end = end + lengths_ref[j]
        start = jnp.where(q_pos >= end, end, start)
        low = jnp.where(first >= end, end, low)
    return start, low // key_rows


def block_place(meta_ref, step, steps, run, tokens_all):
    half = steps // 2
    return (step // half) * (tokens_all // 2) + meta_ref[0] * run + (step % half) * BQ


def head_rows(ref, h, shift):
    part = ref[:, h * HD : (h + 1) * HD]
    zero = jnp.zeros_like(part)
    return jnp.concatenate([zero, part] if shift else [part, zero], axis=1)


def dot_nt(a, b):
    return lax.dot_general(a, b, (((1,), (1,)), ((), ())), preferred_element_type=F32)


def dot_tn(a, b):
    return lax.dot_general(a, b, (((0,), (0,)), ((), ())), preferred_element_type=F32)


def attend_kernel(lengths_ref, meta_ref, q_ref, kv_ref, o_ref, lse_ref, *, segments, planes):
    step = pl.program_id(0)
    steps = pl.num_programs(0)
    rows = kv_ref.shape[1]
    tokens_all = kv_ref.shape[0] * rows
    first = block_place(meta_ref, step, steps, rows, tokens_all)
    q_pos = first + lax.broadcasted_iota(jnp.int32, (1, BQ), 1)
    start, low = doc_ranges(lengths_ref, segments, q_pos, first, rows)
    high = (first + BQ - 1) // rows + 1
    heads = [head_rows(q_ref, h, False) * jnp.asarray(HD**-0.5, BF16) for h in range(GROUP)]

    def visit(block, state):
        part = kv_ref[(block % planes) * 2 + block // planes]
        k_pos = block * rows + lax.broadcasted_iota(jnp.int32, (rows, BQ), 0)
        mask = (k_pos >= start) & (k_pos <= q_pos)
        values = part[:, HD:]
        out = []
        for h in range(GROUP):
            run_max, run_sum, acc = state[h]
            scores = jnp.where(mask, dot_nt(part, heads[h]), NEG)
            new_max = jnp.maximum(run_max, jnp.max(scores, axis=0, keepdims=True))
            shrink = jnp.exp(run_max - new_max)
            weights = jnp.exp(scores - new_max)
            new_sum = run_sum * shrink + jnp.sum(weights, axis=0, keepdims=True)
            acc = acc * shrink + dot_tn(values, weights.astype(BF16))
            out.append((new_max, new_sum, acc))
        return tuple(out)

    begin = tuple(
        (
            jnp.full((1, BQ), NEG, F32),
            jnp.zeros((1, BQ), F32),
            jnp.zeros((HD, BQ), F32),
        )
        for _ in range(GROUP)
    )
    state = lax.fori_loop(low, high, visit, begin)
    o_ref[...] = jnp.concatenate([acc / total for _, total, acc in state], axis=0).T.astype(BF16)
    lse_ref[0] = jnp.concatenate([top + jnp.log(total) for top, total, _ in state], axis=0)


def attend_back_kernel(
    lengths_ref,
    meta_ref,
    q_ref,
    do_ref,
    o_ref,
    lse_ref,
    kv_ref,
    dq_ref,
    dkv_ref,
    acc_ref,
    *,
    segments,
    planes,
):
    step = pl.program_id(0)
    steps = pl.num_programs(0)
    rows = kv_ref.shape[1]
    tokens_all = kv_ref.shape[0] * rows
    first = block_place(meta_ref, step, steps, rows, tokens_all)
    q_pos = first + lax.broadcasted_iota(jnp.int32, (1, BQ), 1)
    start, low = doc_ranges(lengths_ref, segments, q_pos, first, rows)
    high = (first + BQ - 1) // rows + 1
    scale = HD**-0.5

    @pl.when(step == 0)
    def _():
        acc_ref[...] = jnp.zeros_like(acc_ref)

    queries = [head_rows(q_ref, h, False) * jnp.asarray(scale, BF16) for h in range(GROUP)]
    d_outs = [head_rows(do_ref, h, True) for h in range(GROUP)]
    products = (do_ref[...].astype(F32) * o_ref[...].astype(F32)).T
    row_dots = [
        jnp.sum(products[h * HD : (h + 1) * HD], axis=0, keepdims=True) for h in range(GROUP)
    ]
    both = [jnp.concatenate([queries[h], d_outs[h]], axis=0) for h in range(GROUP)]

    def visit(block, state):
        place = (block % planes) * 2 + block // planes
        part = kv_ref[place]
        k_pos = block * rows + lax.broadcasted_iota(jnp.int32, (rows, BQ), 0)
        mask = (k_pos >= start) & (k_pos <= q_pos)
        keys = part[:, :HD]
        total = jnp.zeros((rows, KV), F32)
        out = []
        for h in range(GROUP):
            scores = dot_nt(part, queries[h])
            probs = jnp.where(mask, jnp.exp(scores - lse_ref[0, h : h + 1, :]), 0.0)
            d_probs = dot_nt(part, d_outs[h])
            d_scores = (probs * (d_probs - row_dots[h])).astype(BF16)
            total = total + jnp.dot(
                jnp.concatenate([d_scores, probs.astype(BF16)], axis=1),
                both[h],
                preferred_element_type=F32,
            )
            out.append(state[h] + dot_tn(keys, d_scores))
        acc_ref[place] += total
        return tuple(out)

    begin = tuple(jnp.zeros((HD, BQ), F32) for _ in range(GROUP))
    state = lax.fori_loop(low, high, visit, begin)
    dq_ref[...] = (jnp.concatenate(state, axis=0) * scale).T.astype(BF16)

    @pl.when(step == steps - 1)
    def _():
        dkv_ref[...] = acc_ref[...].astype(BF16)


def attend(lengths, meta, query, kv_blocks, planes):
    rows = query.shape[0]
    steps = rows // BQ
    return pl.pallas_call(
        functools.partial(attend_kernel, segments=lengths.shape[0], planes=planes),
        out_shape=(
            jax.ShapeDtypeStruct((rows, QW), BF16),
            jax.ShapeDtypeStruct((steps, GROUP, BQ), F32),
        ),
        grid_spec=pltpu.PrefetchScalarGridSpec(
            num_scalar_prefetch=2,
            grid=(steps,),
            in_specs=[
                pl.BlockSpec((BQ, QW), lambda i, *_: (i, 0)),
                pl.BlockSpec(kv_blocks.shape, lambda i, *_: (0, 0, 0)),
            ],
            out_specs=[
                pl.BlockSpec((BQ, QW), lambda i, *_: (i, 0)),
                pl.BlockSpec((1, GROUP, BQ), lambda i, *_: (i, 0, 0)),
            ],
        ),
        name="attend",
    )(lengths, meta, query, kv_blocks)


def attend_back(lengths, meta, query, d_out, out, lse, kv_blocks, planes):
    rows = query.shape[0]
    steps = rows // BQ
    return pl.pallas_call(
        functools.partial(attend_back_kernel, segments=lengths.shape[0], planes=planes),
        out_shape=(
            jax.ShapeDtypeStruct((rows, QW), BF16),
            jax.ShapeDtypeStruct(kv_blocks.shape, BF16),
        ),
        grid_spec=pltpu.PrefetchScalarGridSpec(
            num_scalar_prefetch=2,
            grid=(steps,),
            in_specs=[
                pl.BlockSpec((BQ, QW), lambda i, *_: (i, 0)),
                pl.BlockSpec((BQ, QW), lambda i, *_: (i, 0)),
                pl.BlockSpec((BQ, QW), lambda i, *_: (i, 0)),
                pl.BlockSpec((1, GROUP, BQ), lambda i, *_: (i, 0, 0)),
                pl.BlockSpec(kv_blocks.shape, lambda i, *_: (0, 0, 0)),
            ],
            out_specs=[
                pl.BlockSpec((BQ, QW), lambda i, *_: (i, 0)),
                pl.BlockSpec(kv_blocks.shape, lambda i, *_: (0, 0, 0)),
            ],
            scratch_shapes=[pltpu.VMEM(kv_blocks.shape, F32)],
        ),
        name="attend_back",
    )(lengths, meta, query, d_out, out, lse, kv_blocks)


def split_float(value):
    high = value.astype(BF16)
    return high, (value - high.astype(F32)).astype(BF16)


def shards(
    tokens,
    lengths,
    expert_ids,
    w_query,
    w_key,
    w_value,
    w_out,
    w_router,
    gain_attn,
    gain_moe,
    w_gate,
    w_up,
    w_down,
    cotangent,
):
    heads = lax.axis_size("head")
    planes = lax.axis_size("tg")
    members = lax.axis_size("hg")
    blk_count = planes * members
    devices = heads * blk_count
    in_group = heads * members
    tok_dev = tokens.shape[0]
    rows_dev = w_query.shape[0]
    experts = blk_count
    capacity = max(2, 3 * tok_dev // experts)
    slots = experts * capacity
    rows_group = in_group * tok_dev
    run = members * tok_dev
    slab = pad_up(QKV + experts + 1)
    plane = lax.axis_index("tg")
    blk_index = plane * members + lax.axis_index("hg")
    partner = [(i, heads - 1 - i) for i in range(heads)]

    by_group = jnp.concatenate(
        [
            w_query.reshape(rows_dev, in_group, QW),
            w_key.reshape(rows_dev, in_group, HD),
            w_value.reshape(rows_dev, in_group, HD),
            jnp.broadcast_to(gain_attn[:, None, None], (rows_dev, in_group, 1)),
            jnp.zeros((rows_dev, in_group, slab - QKV - 1), BF16),
        ],
        axis=2,
    )
    to_send = by_group.transpose(1, 0, 2).reshape(heads, 1, members, rows_dev, slab)
    to_send = jnp.broadcast_to(to_send, (heads, planes, members, rows_dev, slab))
    own_slab = lax.all_to_all(
        to_send.reshape(devices, rows_dev, slab), ALL, split_axis=0, concat_axis=0, tiled=True
    ).reshape(D, slab)
    x_group = lax.all_gather(tokens, PLANE, axis=0, tiled=True)
    extra = pad_up(experts + 1)
    out_shard = jnp.concatenate(
        [
            w_out,
            w_router,
            gain_moe[:, None],
            jnp.zeros((rows_dev, extra - experts - 1), BF16),
        ],
        axis=1,
    )
    full_out = lax.all_gather(out_shard, ALL, axis=0, tiled=True)
    full_in = lax.all_gather(by_group.reshape(rows_dev, in_group * slab), ALL, axis=0, tiled=True)

    seq_ends = jnp.cumsum(lengths)
    own_pos = (lax.axis_index("head") * blk_count + blk_index) * tok_dev + jnp.arange(
        tok_dev, dtype=jnp.int32
    )
    valid_bool = own_pos < seq_ends[-2]
    valid_float = valid_bool.astype(F32)[:, None]
    pair_experts = expert_ids.reshape(-1)
    live_pairs = jnp.repeat(valid_bool, 2)
    onehot = (
        (pair_experts[:, None] == jnp.arange(experts, dtype=jnp.int32)[None, :])
        & live_pairs[:, None]
    ).astype(jnp.int32)
    earlier = jnp.cumsum(onehot, axis=0) - onehot
    slot_index = jnp.sum(earlier * onehot, axis=1)
    kept_pairs = live_pairs & (slot_index < capacity)
    flat_index = jnp.where(kept_pairs, pair_experts * capacity + slot_index, -1)
    slot_ids = jnp.arange(slots, dtype=jnp.int32)
    slot_bool = flat_index[None, :] == slot_ids[:, None]
    token_index = flat_index.reshape(tok_dev, 2)
    token_table = (
        (token_index[:, 0][:, None] == slot_ids[None, :])
        | (token_index[:, 1][:, None] == slot_ids[None, :])
    ).astype(BF16)
    pick_table = (
        expert_ids[:, :, None] == jnp.arange(experts, dtype=jnp.int32)[None, None, :]
    ).astype(F32)

    def to_experts(rows):
        sent = lax.all_to_all(
            rows.reshape(experts, capacity, rows.shape[1]),
            BLK,
            split_axis=0,
            concat_axis=0,
            tiled=True,
        ).reshape(slots, rows.shape[1])
        return jnp.concatenate([sent, lax.ppermute(sent, "head", partner)], axis=0)

    def to_tokens(partial):
        theirs = lax.ppermute(partial[slots:].astype(BF16), "head", partner)
        summed = (partial[:slots] + theirs.astype(F32)).astype(BF16)
        return lax.all_to_all(
            summed.reshape(experts, capacity, summed.shape[1]),
            BLK,
            split_axis=0,
            concat_axis=0,
            tiled=True,
        ).reshape(slots, summed.shape[1])

    def pick_rows(values):
        return lax.dot_general(
            token_table, values, (((0,), (0,)), ((), ())), preferred_element_type=F32
        )

    x_float = x_group.astype(F32)
    gain_one = own_slab[:, QKV].astype(F32)[None, :]
    normed_one = (x_float * rms_scale(x_float) * gain_one).astype(BF16)
    qkv = jnp.dot(normed_one, own_slab, preferred_element_type=F32).astype(BF16)
    query = qkv[:, :QW]
    kv_own = qkv[:, QW:QKV]
    kv_blocks = lax.all_gather(kv_own, "tg", axis=0, tiled=True).reshape(planes * 2, run, KV)
    meta = plane.astype(jnp.int32).reshape(1)
    attn_rows, lse = attend(lengths, meta, query, kv_blocks, planes)
    attn_tokens = lax.all_to_all(attn_rows, PLANE, split_axis=0, concat_axis=1, tiled=True)

    d_rows = to_experts(pick_rows(cotangent).astype(BF16))

    own_x = tokens.astype(F32)
    hidden_one = own_x + jnp.dot(attn_tokens, full_out[:, :D], preferred_element_type=F32)
    scale_two = rms_scale(hidden_one)
    gain_two = full_out[:, D + experts].astype(F32)[None, :]
    router = full_out[:, D : D + experts]
    normed_two = (hidden_one * scale_two * gain_two).astype(BF16)
    logits = jnp.dot(normed_two, router, preferred_element_type=F32)
    mix = jax.nn.softmax(jnp.sum(pick_table * logits[:, None, :], axis=2), axis=1)
    slot_mix = jnp.sum(jnp.where(slot_bool, mix.reshape(1, -1), 0.0), axis=1, keepdims=True)
    mix_high, mix_low = split_float(slot_mix)
    moe_rows = to_experts(
        jnp.concatenate(
            [
                pick_rows(normed_two).astype(BF16),
                mix_high,
                mix_low,
                jnp.zeros((slots, LANE - 2), BF16),
            ],
            axis=1,
        )
    )

    gate_mat = w_gate[0]
    up_mat = w_up[0]
    down_mat = w_down[0]
    rows = moe_rows[:, :D]
    row_mix = moe_rows[:, D : D + 1].astype(F32) + moe_rows[:, D + 1 : D + 2].astype(F32)
    gate_pre = jnp.dot(rows, gate_mat, preferred_element_type=F32)
    up_pre = jnp.dot(rows, up_mat, preferred_element_type=F32)
    sigmoid_gate = jax.nn.sigmoid(gate_pre)
    inner = gate_pre * sigmoid_gate * up_pre
    inner_act = inner.astype(BF16)
    d_inner = jnp.einsum("rd,fd->rf", d_rows, down_mat, preferred_element_type=F32)
    d_mix_part = jnp.sum(d_inner * inner, axis=1, keepdims=True)
    d_scaled = d_inner * row_mix
    d_gate = (d_scaled * up_pre * sigmoid_gate * (1.0 + gate_pre * (1.0 - sigmoid_gate))).astype(
        BF16
    )
    d_up = (d_scaled * gate_pre * sigmoid_gate).astype(BF16)
    d_in = jnp.einsum("rf,df->rd", d_gate, gate_mat, preferred_element_type=F32) + jnp.einsum(
        "rf,df->rd", d_up, up_mat, preferred_element_type=F32
    )
    mix_part_high, mix_part_low = split_float(d_mix_part)
    d_back = to_tokens(
        jnp.concatenate(
            [
                d_in,
                mix_part_high.astype(F32),
                mix_part_low.astype(F32),
                jnp.zeros((2 * slots, LANE - 2), F32),
            ],
            axis=1,
        )
    )
    y_back = to_tokens(jnp.dot(inner_act, down_mat, preferred_element_type=F32) * row_mix)
    output = (
        valid_float * (hidden_one + jnp.dot(token_table, y_back, preferred_element_type=F32))
    ).astype(BF16)
    d_y = (d_rows.astype(F32) * row_mix).astype(BF16)
    grad_gate = jnp.einsum("rd,rf->df", rows, d_gate, preferred_element_type=F32)[None]
    grad_up = jnp.einsum("rd,rf->df", rows, d_up, preferred_element_type=F32)[None]
    grad_down = jnp.einsum("rf,rd->fd", inner_act, d_y, preferred_element_type=F32)[None]

    d_out = cotangent.astype(F32) * valid_float
    slot_d_mix = d_back[:, D : D + 1].astype(F32) + d_back[:, D + 1 : D + 2].astype(F32)
    d_mix = jnp.sum(jnp.where(slot_bool, slot_d_mix, 0.0), axis=0).reshape(tok_dev, 2)
    d_chosen = mix * (d_mix - jnp.sum(mix * d_mix, axis=1, keepdims=True))
    d_logits = jnp.sum(pick_table * d_chosen[:, :, None], axis=1).astype(BF16)
    grad_router_part = jnp.einsum("td,te->de", normed_two, d_logits, preferred_element_type=F32)
    d_normed_two = jnp.dot(
        token_table, d_back[:, :D], preferred_element_type=F32
    ) + jnp.einsum("te,de->td", d_logits, router, preferred_element_type=F32)
    gain_moe_part = jnp.sum(d_normed_two * hidden_one * scale_two, axis=0)
    along_two = gain_two * d_normed_two
    d_hidden = (
        d_out
        + scale_two * along_two
        - hidden_one
        * (
            scale_two
            * scale_two
            * scale_two
            * jnp.mean(along_two * hidden_one, axis=-1, keepdims=True)
        )
    )
    d_proj = d_hidden.astype(BF16)
    d_attn = jnp.einsum("td,id->ti", d_proj, full_out[:, :D], preferred_element_type=F32).astype(
        BF16
    )
    d_attn_rows = lax.all_to_all(d_attn, PLANE, split_axis=1, concat_axis=0, tiled=True)
    grad_out_part = jnp.einsum("ti,td->id", attn_tokens, d_proj, preferred_element_type=F32)
    grad_out = lax.psum_scatter(
        grad_out_part.astype(BF16), ALL, scatter_dimension=0, tiled=True
    ).astype(F32)

    d_query, d_kv_blocks = attend_back(
        lengths, meta, query, d_attn_rows, attn_rows, lse, kv_blocks, planes
    )
    d_kv_parts = lax.all_to_all(
        d_kv_blocks.reshape(planes, rows_group, KV), "tg", split_axis=0, concat_axis=0, tiled=True
    )
    d_kv = jnp.sum(d_kv_parts.astype(F32), axis=0).astype(BF16)
    d_qkv = jnp.concatenate(
        [d_query, d_kv, jnp.zeros((rows_group, slab - QKV), BF16)], axis=1
    )
    d_tokens = lax.all_to_all(d_qkv, PLANE, split_axis=0, concat_axis=1, tiled=True)
    grad_in = jnp.einsum("td,ti->di", normed_one, d_qkv, preferred_element_type=F32)
    grad_in = jnp.concatenate(
        [
            grad_in[:, :QKV],
            grad_router_part,
            gain_moe_part[:, None],
            jnp.zeros((D, slab - QKV - experts - 1), F32),
        ],
        axis=1,
    ).astype(BF16)
    grad_parts = lax.all_to_all(
        grad_in.reshape(devices, rows_dev, slab), ALL, split_axis=0, concat_axis=0, tiled=True
    ).astype(F32)
    grad_small = jnp.sum(grad_parts[:, :, QKV:], axis=0)
    grad_router = grad_small[:, :experts]
    grad_gain_moe = grad_small[:, experts]
    grad_qkv = jnp.sum(
        grad_parts[:, :, :QKV].reshape(heads, planes, members, rows_dev, QKV), axis=1
    )
    grad_qkv = grad_qkv.reshape(in_group, rows_dev, QKV).transpose(1, 0, 2)
    grad_query = grad_qkv[:, :, :QW].reshape(rows_dev, HQ * HD)
    grad_key = grad_qkv[:, :, QW : QW + HD].reshape(rows_dev, HK * HD)
    grad_value = grad_qkv[:, :, QW + HD :].reshape(rows_dev, HK * HD)
    grad_gain_attn = (
        jnp.sum(grad_qkv * by_group[:, :, :QKV].astype(F32), axis=(1, 2)) / gain_attn.astype(F32)
    )
    d_normed_one = jnp.einsum("ti,di->td", d_tokens, full_in, preferred_element_type=F32)
    scale_one = rms_scale(own_x)
    along_one = gain_one * d_normed_one
    input_grad = (
        d_hidden
        + scale_one * along_one
        - own_x
        * (
            scale_one
            * scale_one
            * scale_one
            * jnp.mean(along_one * own_x, axis=-1, keepdims=True)
        )
    ).astype(BF16)
    return (
        output,
        input_grad,
        grad_query,
        grad_key,
        grad_value,
        grad_out,
        grad_router,
        grad_gain_attn,
        grad_gain_moe,
        grad_gate,
        grad_up,
        grad_down,
    )


def solution(mesh):
    heads = mesh.shape["head"]
    members = HK // heads
    planes = mesh.shape["blk"] // members
    inner = Mesh(mesh.devices.reshape(heads, planes, members), ALL)
    rows = P(ALL, None)
    placed = (
        rows,
        P(),
        rows,
        rows,
        rows,
        rows,
        rows,
        rows,
        P(ALL),
        P(ALL),
        P(BLK, None, "head"),
        P(BLK, None, "head"),
        P(BLK, "head", None),
        rows,
    )
    return jax.shard_map(
        shards,
        mesh=inner,
        in_specs=placed,
        out_specs=(
            rows,
            rows,
            rows,
            rows,
            rows,
            rows,
            rows,
            P(ALL),
            P(ALL),
            P(BLK, None, "head"),
            P(BLK, None, "head"),
            P(BLK, "head", None),
        ),
        check_vma=False,
    )
```

```python
import functools

import jax
import jax.numpy as jnp
from jax import lax
from jax.experimental import pallas as pl
from jax.experimental.pallas import tpu as pltpu
from jax.sharding import Mesh
from jax.sharding import PartitionSpec as P

D = 1536
HQ = 24
HK = 8
HD = 64
GROUP = HQ // HK
QW = GROUP * HD
KV = 2 * HD
QKV = QW + KV
LANE = 128
EPS = 1e-05
NEG = -1e30
BQ = 256
F32 = jnp.float32
BF16 = jnp.bfloat16

PLANE = ("head", "hg")
BLK = ("tg", "hg")
ALL = ("head", "tg", "hg")


def pad_up(count):
    return -(-count // LANE) * LANE


def rms_scale(values):
    return lax.rsqrt(jnp.mean(values * values, axis=-1, keepdims=True) + EPS)


def doc_ranges(lengths_ref, segments, q_pos, first, key_rows):
    start = jnp.zeros_like(q_pos)
    low = jnp.int32(0)
    end = jnp.int32(0)
    for j in range(segments):
        end = end + lengths_ref[j]
        start = jnp.where(q_pos >= end, end, start)
        low = jnp.where(first >= end, end, low)
    return start, low // key_rows


def block_place(meta_ref, step, steps, run, tokens_all):
    half = steps // 2
    return (step // half) * (tokens_all // 2) + meta_ref[0] * run + (step % half) * BQ


def head_rows(ref, h, shift):
    part = ref[:, h * HD : (h + 1) * HD]
    zero = jnp.zeros_like(part)
    return jnp.concatenate([zero, part] if shift else [part, zero], axis=1)


def dot_nt(a, b):
    return lax.dot_general(a, b, (((1,), (1,)), ((), ())), preferred_element_type=F32)


def dot_tn(a, b):
    return lax.dot_general(a, b, (((0,), (0,)), ((), ())), preferred_element_type=F32)


def attend_kernel(lengths_ref, meta_ref, q_ref, kv_ref, o_ref, lse_ref, *, segments, planes):
    step = pl.program_id(0)
    steps = pl.num_programs(0)
    rows = kv_ref.shape[1]
    tokens_all = kv_ref.shape[0] * rows
    first = block_place(meta_ref, step, steps, rows, tokens_all)
    q_pos = first + lax.broadcasted_iota(jnp.int32, (1, BQ), 1)
    start, low = doc_ranges(lengths_ref, segments, q_pos, first, rows)
    high = (first + BQ - 1) // rows + 1
    heads = [head_rows(q_ref, h, False) * jnp.asarray(HD**-0.5, BF16) for h in range(GROUP)]

    def visit(block, state):
        part = kv_ref[(block % planes) * 2 + block // planes]
        k_pos = block * rows + lax.broadcasted_iota(jnp.int32, (rows, BQ), 0)
        mask = (k_pos >= start) & (k_pos <= q_pos)
        values = part[:, HD:]
        out = []
        for h in range(GROUP):
            run_max, run_sum, acc = state[h]
            scores = jnp.where(mask, dot_nt(part, heads[h]), NEG)
            new_max = jnp.maximum(run_max, jnp.max(scores, axis=0, keepdims=True))
            shrink = jnp.exp(run_max - new_max)
            weights = jnp.exp(scores - new_max)
            new_sum = run_sum * shrink + jnp.sum(weights, axis=0, keepdims=True)
            acc = acc * shrink + dot_tn(values, weights.astype(BF16))
            out.append((new_max, new_sum, acc))
        return tuple(out)

    begin = tuple(
        (
            jnp.full((1, BQ), NEG, F32),
            jnp.zeros((1, BQ), F32),
            jnp.zeros((HD, BQ), F32),
        )
        for _ in range(GROUP)
    )
    state = lax.fori_loop(low, high, visit, begin)
    o_ref[...] = jnp.concatenate([acc / total for _, total, acc in state], axis=0).T.astype(BF16)
    lse_ref[0] = jnp.concatenate([top + jnp.log(total) for top, total, _ in state], axis=0)


def attend_back_kernel(
    lengths_ref,
    meta_ref,
    q_ref,
    do_ref,
    o_ref,
    lse_ref,
    kv_ref,
    dq_ref,
    dkv_ref,
    acc_ref,
    *,
    segments,
    planes,
):
    step = pl.program_id(0)
    steps = pl.num_programs(0)
    rows = kv_ref.shape[1]
    tokens_all = kv_ref.shape[0] * rows
    first = block_place(meta_ref, step, steps, rows, tokens_all)
    q_pos = first + lax.broadcasted_iota(jnp.int32, (1, BQ), 1)
    start, low = doc_ranges(lengths_ref, segments, q_pos, first, rows)
    high = (first + BQ - 1) // rows + 1
    scale = HD**-0.5

    @pl.when(step == 0)
    def _():
        acc_ref[...] = jnp.zeros_like(acc_ref)

    queries = [head_rows(q_ref, h, False) * jnp.asarray(scale, BF16) for h in range(GROUP)]
    d_outs = [head_rows(do_ref, h, True) for h in range(GROUP)]
    products = (do_ref[...].astype(F32) * o_ref[...].astype(F32)).T
    row_dots = [
        jnp.sum(products[h * HD : (h + 1) * HD], axis=0, keepdims=True) for h in range(GROUP)
    ]
    both = [jnp.concatenate([queries[h], d_outs[h]], axis=0) for h in range(GROUP)]

    def visit(block, state):
        place = (block % planes) * 2 + block // planes
        part = kv_ref[place]
        k_pos = block * rows + lax.broadcasted_iota(jnp.int32, (rows, BQ), 0)
        mask = (k_pos >= start) & (k_pos <= q_pos)
        keys = part[:, :HD]
        total = jnp.zeros((rows, KV), F32)
        out = []
        for h in range(GROUP):
            scores = dot_nt(part, queries[h])
            probs = jnp.where(mask, jnp.exp(scores - lse_ref[0, h : h + 1, :]), 0.0)
            d_probs = dot_nt(part, d_outs[h])
            d_scores = (probs * (d_probs - row_dots[h])).astype(BF16)
            total = total + jnp.dot(
                jnp.concatenate([d_scores, probs.astype(BF16)], axis=1),
                both[h],
                preferred_element_type=F32,
            )
            out.append(state[h] + dot_tn(keys, d_scores))
        acc_ref[place] += total
        return tuple(out)

    begin = tuple(jnp.zeros((HD, BQ), F32) for _ in range(GROUP))
    state = lax.fori_loop(low, high, visit, begin)
    dq_ref[...] = (jnp.concatenate(state, axis=0) * scale).T.astype(BF16)

    @pl.when(step == steps - 1)
    def _():
        dkv_ref[...] = acc_ref[...].astype(BF16)


def attend(lengths, meta, query, kv_blocks, planes):
    rows = query.shape[0]
    steps = rows // BQ
    return pl.pallas_call(
        functools.partial(attend_kernel, segments=lengths.shape[0], planes=planes),
        out_shape=(
            jax.ShapeDtypeStruct((rows, QW), BF16),
            jax.ShapeDtypeStruct((steps, GROUP, BQ), F32),
        ),
        grid_spec=pltpu.PrefetchScalarGridSpec(
            num_scalar_prefetch=2,
            grid=(steps,),
            in_specs=[
                pl.BlockSpec((BQ, QW), lambda i, *_: (i, 0)),
                pl.BlockSpec(kv_blocks.shape, lambda i, *_: (0, 0, 0)),
            ],
            out_specs=[
                pl.BlockSpec((BQ, QW), lambda i, *_: (i, 0)),
                pl.BlockSpec((1, GROUP, BQ), lambda i, *_: (i, 0, 0)),
            ],
        ),
        name="attend",
    )(lengths, meta, query, kv_blocks)


def attend_back(lengths, meta, query, d_out, out, lse, kv_blocks, planes):
    rows = query.shape[0]
    steps = rows // BQ
    return pl.pallas_call(
        functools.partial(attend_back_kernel, segments=lengths.shape[0], planes=planes),
        out_shape=(
            jax.ShapeDtypeStruct((rows, QW), BF16),
            jax.ShapeDtypeStruct(kv_blocks.shape, BF16),
        ),
        grid_spec=pltpu.PrefetchScalarGridSpec(
            num_scalar_prefetch=2,
            grid=(steps,),
            in_specs=[
                pl.BlockSpec((BQ, QW), lambda i, *_: (i, 0)),
                pl.BlockSpec((BQ, QW), lambda i, *_: (i, 0)),
                pl.BlockSpec((BQ, QW), lambda i, *_: (i, 0)),
                pl.BlockSpec((1, GROUP, BQ), lambda i, *_: (i, 0, 0)),
                pl.BlockSpec(kv_blocks.shape, lambda i, *_: (0, 0, 0)),
            ],
            out_specs=[
                pl.BlockSpec((BQ, QW), lambda i, *_: (i, 0)),
                pl.BlockSpec(kv_blocks.shape, lambda i, *_: (0, 0, 0)),
            ],
            scratch_shapes=[pltpu.VMEM(kv_blocks.shape, F32)],
        ),
        name="attend_back",
    )(lengths, meta, query, d_out, out, lse, kv_blocks)


def split_float(value):
    high = value.astype(BF16)
    return high, (value - high.astype(F32)).astype(BF16)


def shards(
    tokens,
    lengths,
    expert_ids,
    w_query,
    w_key,
    w_value,
    w_out,
    w_router,
    gain_attn,
    gain_moe,
    w_gate,
    w_up,
    w_down,
    cotangent,
):
    heads = lax.axis_size("head")
    planes = lax.axis_size("tg")
    members = lax.axis_size("hg")
    blk_count = planes * members
    devices = heads * blk_count
    in_group = heads * members
    tok_dev = tokens.shape[0]
    rows_dev = w_query.shape[0]
    experts = blk_count
    capacity = max(2, 3 * tok_dev // experts)
    slots = experts * capacity
    rows_group = in_group * tok_dev
    run = members * tok_dev
    slab = pad_up(QKV + experts + 1)
    plane = lax.axis_index("tg")
    blk_index = plane * members + lax.axis_index("hg")
    partner = [(i, heads - 1 - i) for i in range(heads)]

    by_group = jnp.concatenate(
        [
            w_query.reshape(rows_dev, in_group, QW),
            w_key.reshape(rows_dev, in_group, HD),
            w_value.reshape(rows_dev, in_group, HD),
            jnp.broadcast_to(gain_attn[:, None, None], (rows_dev, in_group, 1)),
            jnp.zeros((rows_dev, in_group, slab - QKV - 1), BF16),
        ],
        axis=2,
    )
    to_send = by_group.transpose(1, 0, 2).reshape(heads, 1, members, rows_dev, slab)
    to_send = jnp.broadcast_to(to_send, (heads, planes, members, rows_dev, slab))
    own_slab = lax.all_to_all(
        to_send.reshape(devices, rows_dev, slab), ALL, split_axis=0, concat_axis=0, tiled=True
    ).reshape(D, slab)
    x_group = lax.all_gather(tokens, PLANE, axis=0, tiled=True)
    out_shard = jnp.concatenate(
        [
            w_out,
            w_router,
            gain_moe[:, None],
            jnp.zeros((rows_dev, pad_up(experts + 1) - experts - 1), BF16),
        ],
        axis=1,
    )
    full_out = lax.all_gather(out_shard, ALL, axis=0, tiled=True)

    seq_ends = jnp.cumsum(lengths)
    own_pos = (lax.axis_index("head") * blk_count + blk_index) * tok_dev + jnp.arange(
        tok_dev, dtype=jnp.int32
    )
    valid_bool = own_pos < seq_ends[-2]
    valid_float = valid_bool.astype(F32)[:, None]
    expert_range = jnp.arange(experts, dtype=jnp.int32)
    pair_experts = expert_ids.reshape(-1)
    live_pairs = jnp.repeat(valid_bool, 2)
    onehot = (
        (pair_experts[:, None] == expert_range[None, :]) & live_pairs[:, None]
    ).astype(jnp.int32)
    earlier = jnp.cumsum(onehot, axis=0) - onehot
    slot_index = jnp.sum(earlier * onehot, axis=1)
    kept_pairs = live_pairs & (slot_index < capacity)
    flat_index = jnp.where(kept_pairs, pair_experts * capacity + slot_index, -1)
    slot_ids = jnp.arange(slots, dtype=jnp.int32)
    token_index = flat_index.reshape(tok_dev, 2)
    token_table = (
        (token_index[:, 0][:, None] == slot_ids[None, :])
        | (token_index[:, 1][:, None] == slot_ids[None, :])
    ).astype(BF16)
    picked = (expert_ids[:, 0][:, None] == expert_range[None, :]) | (
        expert_ids[:, 1][:, None] == expert_range[None, :]
    )
    side = pad_up(2 * experts)
    side_zeros = jnp.zeros((tok_dev, side - 2 * experts), BF16)
    side_range = jnp.arange(side, dtype=jnp.int32)
    mine = side_range % experts == blk_index
    mine_high = mine & (side_range < experts)
    mine_low = mine & (side_range >= experts) & (side_range < 2 * experts)

    def exchange(rows):
        return lax.all_to_all(
            rows.reshape(experts, capacity, rows.shape[1]),
            BLK,
            split_axis=0,
            concat_axis=0,
            tiled=True,
        ).reshape(slots, rows.shape[1])

    def with_partner(sent):
        return jnp.concatenate([sent, lax.ppermute(sent, "head", partner)], axis=0)

    def pair_sum(partial):
        theirs = lax.ppermute(partial[slots:].astype(BF16), "head", partner)
        return (partial[:slots] + theirs.astype(F32)).astype(BF16)

    def pick_rows(values):
        return lax.dot_general(
            token_table, values, (((0,), (0,)), ((), ())), preferred_element_type=F32
        ).astype(BF16)

    x_float = x_group.astype(F32)
    gain_one = own_slab[:, QKV].astype(F32)[None, :]
    normed_one = (x_float * rms_scale(x_float) * gain_one).astype(BF16)
    qkv = jnp.dot(normed_one, own_slab, preferred_element_type=F32).astype(BF16)
    query = qkv[:, :QW]
    kv_own = qkv[:, QW:QKV]
    with jax.named_scope("kv_send"):
        kv_blocks = lax.all_to_all(
            jnp.broadcast_to(kv_own[None], (planes, rows_group, KV)),
            "tg",
            split_axis=0,
            concat_axis=0,
            tiled=True,
        ).reshape(planes * 2, run, KV)
    d_send = pick_rows(cotangent)
    d_send, kv_blocks = lax.optimization_barrier((d_send, kv_blocks))
    with jax.named_scope("d_send"):
        d_sent = exchange(d_send)
    meta = plane.astype(jnp.int32).reshape(1)
    with jax.named_scope("attention"):
        attn_rows, lse = attend(lengths, meta, query, kv_blocks, planes)
    attn_tokens = lax.all_to_all(attn_rows, PLANE, split_axis=0, concat_axis=1, tiled=True)

    own_x = tokens.astype(F32)
    hidden_one = own_x + jnp.dot(attn_tokens, full_out[:, :D], preferred_element_type=F32)
    scale_two = rms_scale(hidden_one)
    gain_two = full_out[:, D + experts].astype(F32)[None, :]
    router = full_out[:, D : D + experts]
    normed_two = (hidden_one * scale_two * gain_two).astype(BF16)
    logits = jnp.dot(normed_two, router, preferred_element_type=F32)
    mix = jax.nn.softmax(jnp.where(picked, logits, NEG), axis=1)
    mix_high, mix_low = split_float(mix)
    moe_send = pick_rows(jnp.concatenate([normed_two, mix_high, mix_low, side_zeros], axis=1))
    with jax.named_scope("moe_send"):
        moe_sent = exchange(moe_send)
    moe_rows = with_partner(moe_sent)
    with jax.named_scope("d_swap"):
        d_rows = with_partner(d_sent)

    gate_mat = w_gate[0]
    up_mat = w_up[0]
    down_mat = w_down[0]
    rows = moe_rows[:, :D]
    row_mix = jnp.sum(
        jnp.where(mine_high | mine_low, moe_rows[:, D:].astype(F32), 0.0), axis=1, keepdims=True
    )
    gate_pre = jnp.dot(rows, gate_mat, preferred_element_type=F32)
    up_pre = jnp.dot(rows, up_mat, preferred_element_type=F32)
    sigmoid_gate = jax.nn.sigmoid(gate_pre)
    inner = gate_pre * sigmoid_gate * up_pre
    inner_act = inner.astype(BF16)
    d_inner = jnp.einsum("rd,fd->rf", d_rows, down_mat, preferred_element_type=F32)
    d_mix_part = jnp.sum(d_inner * inner, axis=1, keepdims=True)
    d_scaled = d_inner * row_mix
    d_gate = (d_scaled * up_pre * sigmoid_gate * (1.0 + gate_pre * (1.0 - sigmoid_gate))).astype(
        BF16
    )
    d_up = (d_scaled * gate_pre * sigmoid_gate).astype(BF16)
    d_in = jnp.einsum("rf,df->rd", d_gate, gate_mat, preferred_element_type=F32) + jnp.einsum(
        "rf,df->rd", d_up, up_mat, preferred_element_type=F32
    )
    mix_part_high, mix_part_low = split_float(d_mix_part)
    side_back = jnp.where(
        mine_high, mix_part_high, jnp.where(mine_low, mix_part_low, jnp.zeros((), BF16))
    )
    d_sum = pair_sum(d_in)
    side_sum = side_back[:slots].astype(F32) + lax.ppermute(
        side_back[slots:], "head", partner
    ).astype(F32)
    d_mix_high, d_mix_low = split_float(jnp.sum(side_sum, axis=1, keepdims=True))
    side_own = jnp.where(
        mine_high, d_mix_high, jnp.where(mine_low, d_mix_low, jnp.zeros((), BF16))
    )
    with jax.named_scope("moe_back"):
        d_back = exchange(jnp.concatenate([d_sum, side_own], axis=1))
    y_send = pair_sum(jnp.dot(inner_act, down_mat, preferred_element_type=F32) * row_mix)
    d_y = (d_rows.astype(F32) * row_mix).astype(BF16)
    with jax.named_scope("expert_grads"):
        grad_gate = jnp.einsum("rd,rf->df", rows, d_gate, preferred_element_type=F32)[None]
        grad_up = jnp.einsum("rd,rf->df", rows, d_up, preferred_element_type=F32)[None]
        grad_down = jnp.einsum("rf,rd->fd", inner_act, d_y, preferred_element_type=F32)[None]

    d_out = cotangent.astype(F32) * valid_float
    d_token = jnp.dot(token_table, d_back, preferred_element_type=F32)
    d_mix = d_token[:, D : D + experts] + d_token[:, D + experts : D + 2 * experts]
    d_logits = (mix * (d_mix - jnp.sum(mix * d_mix, axis=1, keepdims=True))).astype(BF16)
    grad_router_part = jnp.einsum("td,te->de", normed_two, d_logits, preferred_element_type=F32)
    d_normed_two = d_token[:, :D] + jnp.einsum(
        "te,de->td", d_logits, router, preferred_element_type=F32
    )
    gain_moe_part = jnp.sum(d_normed_two * hidden_one * scale_two, axis=0)
    along_two = gain_two * d_normed_two
    d_hidden = (
        d_out
        + scale_two * along_two
        - hidden_one
        * (
            scale_two
            * scale_two
            * scale_two
            * jnp.mean(along_two * hidden_one, axis=-1, keepdims=True)
        )
    )
    d_proj = d_hidden.astype(BF16)
    d_attn = jnp.einsum("td,id->ti", d_proj, full_out[:, :D], preferred_element_type=F32).astype(
        BF16
    )
    d_attn_rows = lax.all_to_all(d_attn, PLANE, split_axis=1, concat_axis=0, tiled=True)
    grad_out_part = jnp.einsum(
        "ti,td->id", attn_tokens, d_proj, preferred_element_type=F32
    ).astype(BF16)
    grad_out_part, d_attn_rows = lax.optimization_barrier((grad_out_part, d_attn_rows))
    with jax.named_scope("grad_out"):
        grad_out = lax.psum_scatter(
            grad_out_part, ALL, scatter_dimension=0, tiled=True
        ).astype(F32)
    y_send, d_attn_rows = lax.optimization_barrier((y_send, d_attn_rows))
    with jax.named_scope("y_send"):
        y_back = exchange(y_send)
    output = (
        valid_float * (hidden_one + jnp.dot(token_table, y_back, preferred_element_type=F32))
    ).astype(BF16)

    with jax.named_scope("attention_back"):
        d_query, d_kv_blocks = attend_back(
            lengths, meta, query, d_attn_rows, attn_rows, lse, kv_blocks, planes
        )
    d_kv_parts = lax.all_to_all(
        d_kv_blocks.reshape(planes, rows_group, KV), "tg", split_axis=0, concat_axis=0, tiled=True
    )
    d_kv = jnp.sum(d_kv_parts.astype(F32), axis=0).astype(BF16)
    d_qkv = jnp.concatenate(
        [d_query, d_kv, jnp.zeros((rows_group, slab - QKV), BF16)], axis=1
    )
    grad_in = jnp.einsum("td,ti->di", normed_one, d_qkv, preferred_element_type=F32)
    grad_in = jnp.concatenate(
        [
            grad_in[:, :QKV],
            grad_router_part,
            gain_moe_part[:, None],
            jnp.zeros((D, slab - QKV - experts - 1), F32),
        ],
        axis=1,
    ).astype(BF16)
    with jax.named_scope("grad_send"):
        grad_parts = lax.all_to_all(
            grad_in.reshape(devices, rows_dev, slab), ALL, split_axis=0, concat_axis=0, tiled=True
        )
    d_normed_part = jnp.einsum("ti,di->td", d_qkv, own_slab, preferred_element_type=F32)
    with jax.named_scope("d_normed"):
        d_normed_one = lax.psum_scatter(
            d_normed_part.astype(BF16), PLANE, scatter_dimension=0, tiled=True
        ).astype(F32)
    grad_parts = grad_parts.astype(F32)
    grad_small = jnp.sum(grad_parts[:, :, QKV:], axis=0)
    grad_router = grad_small[:, :experts]
    grad_gain_moe = grad_small[:, experts]
    grad_qkv = jnp.sum(
        grad_parts[:, :, :QKV].reshape(heads, planes, members, rows_dev, QKV), axis=1
    )
    grad_qkv = grad_qkv.reshape(in_group, rows_dev, QKV).transpose(1, 0, 2)
    grad_query = grad_qkv[:, :, :QW].reshape(rows_dev, HQ * HD)
    grad_key = grad_qkv[:, :, QW : QW + HD].reshape(rows_dev, HK * HD)
    grad_value = grad_qkv[:, :, QW + HD :].reshape(rows_dev, HK * HD)
    grad_gain_attn = (
        jnp.sum(grad_qkv * by_group[:, :, :QKV].astype(F32), axis=(1, 2)) / gain_attn.astype(F32)
    )
    scale_one = rms_scale(own_x)
    along_one = gain_one * d_normed_one
    input_grad = (
        d_hidden
        + scale_one * along_one
        - own_x
        * (
            scale_one
            * scale_one
            * scale_one
            * jnp.mean(along_one * own_x, axis=-1, keepdims=True)
        )
    ).astype(BF16)
    return (
        output,
        input_grad,
        grad_query,
        grad_key,
        grad_value,
        grad_out,
        grad_router,
        grad_gain_attn,
        grad_gain_moe,
        grad_gate,
        grad_up,
        grad_down,
    )


def solution(mesh):
    heads = mesh.shape["head"]
    members = HK // heads
    planes = mesh.shape["blk"] // members
    inner = Mesh(mesh.devices.reshape(heads, planes, members), ALL)
    rows = P(ALL, None)
    placed = (
        rows,
        P(),
        rows,
        rows,
        rows,
        rows,
        rows,
        rows,
        P(ALL),
        P(ALL),
        P(BLK, None, "head"),
        P(BLK, None, "head"),
        P(BLK, "head", None),
        rows,
    )
    return jax.shard_map(
        shards,
        mesh=inner,
        in_specs=placed,
        out_specs=(
            rows,
            rows,
            rows,
            rows,
            rows,
            rows,
            rows,
            P(ALL),
            P(ALL),
            P(BLK, None, "head"),
            P(BLK, None, "head"),
            P(BLK, "head", None),
        ),
        check_vma=False,
    )
```

```python
import functools

import jax
import jax.numpy as jnp
from jax import lax
from jax.experimental import pallas as pl
from jax.experimental.pallas import tpu as pltpu
from jax.sharding import Mesh
from jax.sharding import PartitionSpec as P


D = 1536
HQ = 24
HK = 8
HD = 64
GROUP = HQ // HK
QW = GROUP * HD
KV = 2 * HD
QKV = QW + KV
LANE = 128
EPS = 1e-05
NEG = -1e30
BQ = 128
KEYS = 256
WIDTHS = (4, 2, 1)
F32 = jnp.float32
BF16 = jnp.bfloat16

TEAM = ("head", "hg")
BLK = ("hg", "tg")
ALL = ("head", "hg", "tg")


def pad_up(count):
    return -(-count // LANE) * LANE


def rms_scale(values):
    return lax.rsqrt(jnp.mean(values * values, axis=-1, keepdims=True) + EPS)


def doc_ranges(lengths_ref, segments, q_pos, first):
    start = jnp.zeros_like(q_pos)
    low = jnp.int32(0)
    end = jnp.int32(0)
    for j in range(segments):
        end = end + lengths_ref[j]
        start = jnp.where(q_pos >= end, end, start)
        low = jnp.where(first >= end, end, low)
    return start, low // KEYS


def head_rows(rows, h, shift):
    part = rows[:, h * HD : (h + 1) * HD]
    zero = jnp.zeros_like(part)
    return jnp.concatenate([zero, part] if shift else [part, zero], axis=1)


def dot_nt(a, b):
    return lax.dot_general(a, b, (((1,), (1,)), ((), ())), preferred_element_type=F32)


def dot_tn(a, b):
    return lax.dot_general(a, b, (((0,), (0,)), ((), ())), preferred_element_type=F32)


def key_place(block, parts, planes):
    first = block * parts
    return [((first + t) % planes, (first + t) // planes) for t in range(parts)]


def allowed_keys(block, start, q_pos):
    k_pos = block * KEYS + lax.broadcasted_iota(jnp.int32, (KEYS, BQ), 0)
    mask = (k_pos >= start) & (k_pos <= q_pos)
    return jnp.concatenate([mask] * GROUP, axis=1)


def in_widths(widths, low, high, visit, state):
    base = low
    for width in widths:
        turns = (high - base) // width
        state = lax.fori_loop(0, turns, functools.partial(visit, width, base), state)
        base = base + turns * width
    return state


def attend_kernel(lengths_ref, meta_ref, q_ref, kv_ref, o_ref, lse_ref, *, segments):
    planes = kv_ref.shape[0]

    def one(step, carry):
        first = (step * planes + meta_ref[0]) * BQ
        rows = pl.ds(pl.multiple_of(step * BQ, BQ), BQ)
        q_pos = first + lax.broadcasted_iota(jnp.int32, (1, BQ), 1)
        start, low = doc_ranges(lengths_ref, segments, q_pos, first)
        high = (first + BQ - 1) // KEYS + 1
        q_part = q_ref[rows, :]
        queries = jnp.concatenate([head_rows(q_part, h, False) for h in range(GROUP)], axis=0)
        queries = queries * jnp.asarray(HD**-0.5, BF16)

        def visit(width, base, turn, state):
            run_max, run_sum, acc = state
            parts = []
            scores = []
            for u in range(width):
                block = base + turn * width + u
                places = key_place(block, KEYS // BQ, planes)
                part = jnp.concatenate([kv_ref[p, r] for p, r in places], axis=0)
                mask = allowed_keys(block, start, q_pos)
                parts.append(part[:, HD:])
                scores.append(jnp.where(mask, dot_nt(part, queries), NEG))
            new_max = run_max
            for value in scores:
                new_max = jnp.maximum(new_max, jnp.max(value, axis=0, keepdims=True))
            shrink = jnp.exp(run_max - new_max)
            run_sum = run_sum * shrink
            acc = acc * shrink
            for part, value in zip(parts, scores):
                weights = jnp.exp(value - new_max)
                run_sum = run_sum + jnp.sum(weights, axis=0, keepdims=True)
                acc = acc + dot_tn(part, weights.astype(BF16))
            return new_max, run_sum, acc

        begin = (
            jnp.full((1, GROUP * BQ), NEG, F32),
            jnp.zeros((1, GROUP * BQ), F32),
            jnp.zeros((HD, GROUP * BQ), F32),
        )
        top, total, acc = in_widths(WIDTHS, low, high, visit, begin)
        out = acc / total
        o_ref[rows, :] = jnp.concatenate(
            [out[:, h * BQ : (h + 1) * BQ] for h in range(GROUP)], axis=0
        ).T.astype(BF16)
        lse_ref[step] = top + jnp.log(total)
        return carry

    lax.fori_loop(0, q_ref.shape[0] // BQ, one, 0)


def attend_back_kernel(
    lengths_ref,
    meta_ref,
    q_ref,
    do_ref,
    o_ref,
    lse_ref,
    kv_ref,
    dq_ref,
    dkv_ref,
    acc_ref,
    *,
    segments,
):
    planes = kv_ref.shape[0]
    scale = HD**-0.5
    acc_ref[...] = jnp.zeros_like(acc_ref)

    def one(step, carry):
        first = (step * planes + meta_ref[0]) * BQ
        rows = pl.ds(pl.multiple_of(step * BQ, BQ), BQ)
        q_pos = first + lax.broadcasted_iota(jnp.int32, (1, BQ), 1)
        start, low = doc_ranges(lengths_ref, segments, q_pos, first)
        high = (first + BQ - 1) // KEYS + 1
        q_part = q_ref[rows, :]
        do_part = do_ref[rows, :]
        queries = jnp.concatenate([head_rows(q_part, h, False) for h in range(GROUP)], axis=0)
        queries = queries * jnp.asarray(scale, BF16)
        d_outs = jnp.concatenate([head_rows(do_part, h, True) for h in range(GROUP)], axis=0)
        products = (do_part.astype(F32) * o_ref[rows, :].astype(F32)).T
        row_dots = jnp.concatenate(
            [
                jnp.sum(products[h * HD : (h + 1) * HD], axis=0, keepdims=True)
                for h in range(GROUP)
            ],
            axis=1,
        )
        both = jnp.concatenate([queries, d_outs], axis=0)
        lse = lse_ref[step]

        def visit(width, base, turn, d_query):
            total = []
            for u in range(width):
                block = base + turn * width + u
                places = key_place(block, KEYS // BQ, planes)
                part = jnp.concatenate([kv_ref[p, r] for p, r in places], axis=0)
                mask = allowed_keys(block, start, q_pos)
                probs = jnp.where(mask, jnp.exp(dot_nt(part, queries) - lse), 0.0)
                d_scores = (probs * (dot_nt(part, d_outs) - row_dots)).astype(BF16)
                value = jnp.dot(
                    jnp.concatenate([d_scores, probs.astype(BF16)], axis=1),
                    both,
                    preferred_element_type=F32,
                )
                total.append((places, value))
                d_query = d_query + dot_tn(part[:, :HD], d_scores)
            for places, value in total:
                for t, (p, r) in enumerate(places):
                    acc_ref[p, r] += value[t * BQ : (t + 1) * BQ]
            return d_query

        begin = jnp.zeros((HD, GROUP * BQ), F32)
        d_query = in_widths(WIDTHS, low, high, visit, begin) * scale
        dq_ref[rows, :] = jnp.concatenate(
            [d_query[:, h * BQ : (h + 1) * BQ] for h in range(GROUP)], axis=0
        ).T.astype(BF16)
        return carry

    lax.fori_loop(0, q_ref.shape[0] // BQ, one, 0)
    dkv_ref[...] = acc_ref[...].astype(BF16)


def vmem_specs(count):
    return [pl.BlockSpec(memory_space=pltpu.SMEM)] * 2 + [
        pl.BlockSpec(memory_space=pltpu.VMEM)
    ] * count


def attend(lengths, meta, query, kv_all):
    rows = query.shape[0]
    return pl.pallas_call(
        functools.partial(attend_kernel, segments=lengths.shape[0]),
        out_shape=(
            jax.ShapeDtypeStruct((rows, QW), BF16),
            jax.ShapeDtypeStruct((rows // BQ, 1, GROUP * BQ), F32),
        ),
        in_specs=vmem_specs(2),
        name="attend",
    )(lengths, meta, query, kv_all)


def attend_back(lengths, meta, query, d_out, out, lse, kv_all):
    rows = query.shape[0]
    return pl.pallas_call(
        functools.partial(attend_back_kernel, segments=lengths.shape[0]),
        out_shape=(
            jax.ShapeDtypeStruct((rows, QW), BF16),
            jax.ShapeDtypeStruct(kv_all.shape, BF16),
        ),
        in_specs=vmem_specs(5),
        scratch_shapes=[pltpu.VMEM(kv_all.shape, F32)],
        name="attend_back",
    )(lengths, meta, query, d_out, out, lse, kv_all)


def project_kernel(place_ref, *refs, members):
    pieces = refs[: 2 * (2 * members - 1)]
    slab_ref, normed_ref, q_ref, kv_ref, weight_ref, gain_ref, x_ref, sems = refs[len(pieces) :]
    planes, team, rows, _ = slab_ref.shape
    member, head = place_ref[0], place_ref[1]
    copies = []
    for side in range(2):
        for shift in range(1 - members, members):
            index = len(copies)
            block = member + shift
            fits = (block >= 0) & (block < members)
            row = jnp.clip(jnp.abs(side - head) * members + block, 0, team - 1) * BQ
            copy = pltpu.make_async_copy(
                pieces[index], x_ref.at[pl.ds(pl.multiple_of(row, BQ), BQ), :], sems.at[index]
            )
            copies.append((fits, copy))
    for fits, copy in copies:
        pl.when(fits)(copy.start)
    for g in range(team):
        for p in range(planes):
            at = (g * planes + p) * rows
            weight_ref[at : at + rows, :] = slab_ref[p, g]
    low = QKV // LANE * LANE
    side = weight_ref[:, low : low + LANE].astype(F32).T
    gain_ref[...] = side[QKV - low : QKV - low + 1]
    for fits, copy in copies:
        pl.when(fits)(copy.wait)

    def one(step, carry):
        block = pl.ds(pl.multiple_of(step * 2 * BQ, 2 * BQ), 2 * BQ)
        x = x_ref[block, :].astype(F32)
        normed = (x * rms_scale(x) * gain_ref[...]).astype(BF16)
        normed_ref[block, :] = normed
        qkv = jnp.dot(normed, weight_ref[...], preferred_element_type=F32).astype(BF16)
        q_ref[block, :] = qkv[:, :QW]
        for p in range(planes):
            kv_ref[p, block, :] = qkv[:, QW:QKV]
        return carry

    lax.fori_loop(0, x_ref.shape[0] // (2 * BQ), one, 0)


def project(place, pieces, slab, members):
    planes, team, _, width = slab.shape
    rows = team * BQ
    return pl.pallas_call(
        functools.partial(project_kernel, members=members),
        out_shape=(
            jax.ShapeDtypeStruct((rows, D), BF16),
            jax.ShapeDtypeStruct((rows, QW), BF16),
            jax.ShapeDtypeStruct((planes, rows, KV), BF16),
            jax.ShapeDtypeStruct((D, width), BF16),
            jax.ShapeDtypeStruct((1, D), F32),
        ),
        in_specs=[pl.BlockSpec(memory_space=pltpu.SMEM)]
        + [pl.BlockSpec(memory_space=pl.ANY)] * len(pieces)
        + [pl.BlockSpec(memory_space=pltpu.VMEM)],
        scratch_shapes=[
            pltpu.VMEM((rows, D), BF16),
            pltpu.SemaphoreType.DMA((len(pieces),)),
        ],
        name="project",
    )(place, *pieces, slab)


def line_gather(rows, members, partner):
    own = {0: rows}
    other = {}
    up = down = rows
    other[0] = lax.ppermute(rows, "head", partner)
    last = members - 1
    for turn in range(last):
        up = lax.ppermute(up, "hg", [(m, m + 1) for m in range(turn, last)])
        down = lax.ppermute(down, "hg", [(m, m - 1) for m in range(last - turn, 0, -1)])
        up, down = lax.optimization_barrier((up, down))
        own[-1 - turn], own[1 + turn] = up, down
        other[-1 - turn] = lax.ppermute(up, "head", partner)
        other[1 + turn] = lax.ppermute(down, "head", partner)
    order = range(-last, members)
    return [own[k] for k in order] + [other[k] for k in order]


def row_of(weights, values):
    return lax.dot_general(
        weights,
        values,
        (((1,), (1,)), ((), ())),
        precision=lax.Precision.HIGHEST,
        preferred_element_type=F32,
    )[:1]


def finish_kernel(parts_ref, slab_ref, q_ref, k_ref, v_ref, router_ref, attn_ref, moe_ref):
    rows, experts = router_ref.shape
    width = slab_ref.shape[2] - QKV
    small = jnp.zeros((rows, width), F32)
    along = jnp.zeros((rows, QKV), F32)
    for g in range(HK):
        part = parts_ref[g].astype(F32)
        q_ref[:, g * QW : (g + 1) * QW] = part[:, :QW]
        k_ref[:, g * HD : (g + 1) * HD] = part[:, QW : QW + HD]
        v_ref[:, g * HD : (g + 1) * HD] = part[:, QW + HD : QKV]
        along += part[:, :QKV] * slab_ref[:, g, :QKV].astype(F32)
        small += part[:, QKV:]
    router_ref[...] = small[:, :experts]
    column = lax.broadcasted_iota(jnp.int32, (8, width), 1)
    moe_ref[...] = row_of((column == experts).astype(F32), small)
    gain = row_of((column == 0).astype(F32), slab_ref[:, 0, QKV:].astype(F32))
    attn_ref[...] = row_of(jnp.ones((8, QKV), F32), along) / gain


def finish_grads(parts, by_group, experts):
    rows = by_group.shape[0]

    def shape(columns):
        return jax.ShapeDtypeStruct((rows, columns), F32)

    line = jax.ShapeDtypeStruct((1, rows), F32)
    out = pl.pallas_call(
        finish_kernel,
        out_shape=(
            shape(HQ * HD),
            shape(HK * HD),
            shape(HK * HD),
            shape(experts),
            line,
            line,
        ),
        name="finish_grads",
    )(parts, by_group)
    return out[:4] + (out[4].reshape(rows), out[5].reshape(rows))


def merge_kernel(turn_ref, dq_ref, parts_ref, slab_ref, qkv_ref, out_ref):
    d_kv = jnp.sum(parts_ref[...].astype(F32), axis=0).astype(BF16)
    zero = jnp.zeros((d_kv.shape[0], qkv_ref.shape[1] - QKV), BF16)
    qkv_ref[...] = jnp.concatenate([dq_ref[...], d_kv, zero], axis=1)
    rows = out_ref.shape[0]
    part = qkv_ref[pl.ds(pl.multiple_of(turn_ref[0] * rows, rows), rows), :]
    out_ref[...] = dot_nt(part, slab_ref[...]).astype(BF16)


def merge_back(turn, d_query, d_kv_parts, slab, heads):
    rows = d_query.shape[0]
    return pl.pallas_call(
        merge_kernel,
        out_shape=(
            jax.ShapeDtypeStruct((rows, slab.shape[1]), BF16),
            jax.ShapeDtypeStruct((rows // heads, D), BF16),
        ),
        in_specs=[
            pl.BlockSpec(memory_space=pltpu.SMEM),
            pl.BlockSpec(memory_space=pltpu.VMEM),
            pl.BlockSpec(memory_space=pltpu.VMEM),
            pl.BlockSpec(memory_space=pltpu.VMEM),
        ],
        name="merge_back",
    )(turn, d_query, d_kv_parts, slab)


def slab_back_kernel(turn_ref, qkv_ref, slab_ref, out_ref):
    rows = out_ref.shape[0]
    part = qkv_ref[pl.ds(pl.multiple_of(turn_ref[0] * rows, rows), rows), :]
    out_ref[...] = dot_nt(part, slab_ref[...]).astype(BF16)


def slab_back(turn, d_qkv, slab, heads):
    return pl.pallas_call(
        slab_back_kernel,
        out_shape=jax.ShapeDtypeStruct((d_qkv.shape[0] // heads, D), BF16),
        in_specs=[
            pl.BlockSpec(memory_space=pltpu.SMEM),
            pl.BlockSpec(memory_space=pltpu.VMEM),
            pl.BlockSpec(memory_space=pltpu.VMEM),
        ],
        name="slab_back",
    )(turn, d_qkv, slab)


def line_sum(parts, place):
    last = parts.shape[0] - 1
    up = jnp.zeros(parts.shape[1:], BF16)
    down = jnp.zeros(parts.shape[1:], BF16)

    def block(index):
        return lax.dynamic_index_in_dim(parts, jnp.clip(index, 0, last), 0, keepdims=False)

    for turn in range(last):
        to_up = block(place + last - turn)
        to_down = block(place - last + turn)
        if turn:
            to_up = (to_up.astype(F32) + up.astype(F32)).astype(BF16)
            to_down = (to_down.astype(F32) + down.astype(F32)).astype(BF16)
        up = lax.ppermute(to_up, "hg", [(m, m + 1) for m in range(turn + 1)])
        down = lax.ppermute(to_down, "hg", [(m, m - 1) for m in range(last, last - turn - 1, -1)])
        up, down = lax.optimization_barrier((up, down))
    return block(place).astype(F32) + up.astype(F32) + down.astype(F32)


def split_float(value):
    high = value.astype(BF16)
    return high, (value - high.astype(F32)).astype(BF16)


def shards(
    tokens,
    lengths,
    expert_ids,
    w_query,
    w_key,
    w_value,
    w_out,
    w_router,
    gain_attn,
    gain_moe,
    w_gate,
    w_up,
    w_down,
    cotangent,
):
    heads = lax.axis_size("head")
    planes = lax.axis_size("tg")
    members = lax.axis_size("hg")
    blk_count = planes * members
    in_group = heads * members
    tok_dev = tokens.shape[0]
    rows_dev = w_query.shape[0]
    experts = blk_count
    capacity = max(2, 3 * tok_dev // experts)
    slots = experts * capacity
    rows_group = in_group * tok_dev
    slab = pad_up(QKV + experts + 1)
    plane = lax.axis_index("tg")
    member = lax.axis_index("hg")
    blk_index = member * planes + plane
    partner = [(i, heads - 1 - i) for i in range(heads)]

    by_group = jnp.concatenate(
        [
            w_query.reshape(rows_dev, in_group, QW),
            w_key.reshape(rows_dev, in_group, HD),
            w_value.reshape(rows_dev, in_group, HD),
            jnp.broadcast_to(gain_attn[:, None, None], (rows_dev, in_group, 1)),
            jnp.zeros((rows_dev, in_group, slab - QKV - 1), BF16),
        ],
        axis=2,
    )
    slab_team = lax.all_to_all(
        by_group.transpose(1, 0, 2), TEAM, split_axis=0, concat_axis=0, tiled=True
    )
    own_slab = lax.all_to_all(
        jnp.broadcast_to(slab_team[None], (planes, in_group, rows_dev, slab)),
        "tg",
        split_axis=0,
        concat_axis=0,
        tiled=True,
    )
    pieces = line_gather(tokens, members, partner)
    out_shard = jnp.concatenate(
        [
            w_out,
            w_router,
            gain_moe[:, None],
            jnp.zeros((rows_dev, pad_up(experts + 1) - experts - 1), BF16),
        ],
        axis=1,
    )
    full_out = lax.all_gather(out_shard, ALL, axis=0, tiled=True)

    seq_ends = jnp.cumsum(lengths)
    own_pos = (lax.axis_index("head") * blk_count + blk_index) * tok_dev + jnp.arange(
        tok_dev, dtype=jnp.int32
    )
    valid_bool = own_pos < seq_ends[-2]
    valid_float = valid_bool.astype(F32)[:, None]
    expert_range = jnp.arange(experts, dtype=jnp.int32)
    pair_experts = expert_ids.reshape(-1)
    live_pairs = jnp.repeat(valid_bool, 2)
    onehot = (
        (pair_experts[:, None] == expert_range[None, :]) & live_pairs[:, None]
    ).astype(jnp.int32)
    earlier = jnp.cumsum(onehot, axis=0) - onehot
    slot_index = jnp.sum(earlier * onehot, axis=1)
    kept_pairs = live_pairs & (slot_index < capacity)
    flat_index = jnp.where(kept_pairs, pair_experts * capacity + slot_index, -1)
    slot_ids = jnp.arange(slots, dtype=jnp.int32)
    token_index = flat_index.reshape(tok_dev, 2)
    token_table = (
        (token_index[:, 0][:, None] == slot_ids[None, :])
        | (token_index[:, 1][:, None] == slot_ids[None, :])
    ).astype(BF16)
    picked = (expert_ids[:, 0][:, None] == expert_range[None, :]) | (
        expert_ids[:, 1][:, None] == expert_range[None, :]
    )
    side = pad_up(2 * experts)
    side_zeros = jnp.zeros((tok_dev, side - 2 * experts), BF16)
    side_range = jnp.arange(side, dtype=jnp.int32)
    mine = side_range % experts == blk_index
    mine_high = mine & (side_range < experts)
    mine_low = mine & (side_range >= experts) & (side_range < 2 * experts)

    def exchange(rows):
        return lax.all_to_all(
            rows.reshape(experts, capacity, rows.shape[1]),
            BLK,
            split_axis=0,
            concat_axis=0,
            tiled=True,
        ).reshape(slots, rows.shape[1])

    def with_partner(sent):
        return jnp.concatenate([sent, lax.ppermute(sent, "head", partner)], axis=0)

    def pair_sum(partial):
        theirs = lax.ppermute(partial[slots:].astype(BF16), "head", partner)
        return (partial[:slots] + theirs.astype(F32)).astype(BF16)

    def pick_rows(values):
        return lax.dot_general(
            token_table, values, (((0,), (0,)), ((), ())), preferred_element_type=F32
        ).astype(BF16)

    normed_one, query, kv_copies, own_slab, gain_one = project(
        jnp.stack([member, lax.axis_index("head")]).astype(jnp.int32), pieces, own_slab, members
    )
    kv_all = lax.all_to_all(
        kv_copies, "tg", split_axis=0, concat_axis=0, tiled=True
    ).reshape(planes, in_group, tok_dev, KV)
    d_send = pick_rows(cotangent)
    d_send, kv_all = lax.optimization_barrier((d_send, kv_all))
    d_sent = exchange(d_send)
    meta = plane.astype(jnp.int32).reshape(1)
    attn_rows, lse = attend(lengths, meta, query, kv_all)
    d_sent, attn_rows = lax.optimization_barrier((d_sent, attn_rows))
    attn_tokens = lax.all_to_all(attn_rows, TEAM, split_axis=0, concat_axis=1, tiled=True)

    own_x = tokens.astype(F32)
    hidden_one = own_x + jnp.dot(attn_tokens, full_out[:, :D], preferred_element_type=F32)
    scale_two = rms_scale(hidden_one)
    gain_two = full_out[:, D + experts].astype(F32)[None, :]
    router = full_out[:, D : D + experts]
    normed_two = (hidden_one * scale_two * gain_two).astype(BF16)
    logits = jnp.dot(normed_two, router, preferred_element_type=F32)
    mix = jax.nn.softmax(jnp.where(picked, logits, NEG), axis=1)
    mix_high, mix_low = split_float(mix)
    moe_send = pick_rows(jnp.concatenate([normed_two, mix_high, mix_low, side_zeros], axis=1))
    moe_sent = exchange(moe_send)
    moe_rows = with_partner(moe_sent)
    d_rows = with_partner(d_sent)

    gate_mat = w_gate[0]
    up_mat = w_up[0]
    down_mat = w_down[0]
    rows = moe_rows[:, :D]
    row_mix = jnp.sum(
        jnp.where(mine_high | mine_low, moe_rows[:, D:].astype(F32), 0.0), axis=1, keepdims=True
    )
    gate_pre = jnp.dot(rows, gate_mat, preferred_element_type=F32)
    up_pre = jnp.dot(rows, up_mat, preferred_element_type=F32)
    sigmoid_gate = jax.nn.sigmoid(gate_pre)
    inner = gate_pre * sigmoid_gate * up_pre
    inner_act = inner.astype(BF16)
    d_inner = jnp.einsum("rd,fd->rf", d_rows, down_mat, preferred_element_type=F32)
    d_mix_part = jnp.sum(d_inner * inner, axis=1, keepdims=True)
    d_scaled = d_inner * row_mix
    d_gate = (d_scaled * up_pre * sigmoid_gate * (1.0 + gate_pre * (1.0 - sigmoid_gate))).astype(
        BF16
    )
    d_up = (d_scaled * gate_pre * sigmoid_gate).astype(BF16)
    d_in = jnp.einsum("rf,df->rd", d_gate, gate_mat, preferred_element_type=F32) + jnp.einsum(
        "rf,df->rd", d_up, up_mat, preferred_element_type=F32
    )
    mix_part_high, mix_part_low = split_float(d_mix_part)
    side_back = jnp.where(
        mine_high, mix_part_high, jnp.where(mine_low, mix_part_low, jnp.zeros((), BF16))
    )
    d_sum = pair_sum(d_in)
    side_sum = side_back[:slots].astype(F32) + lax.ppermute(
        side_back[slots:], "head", partner
    ).astype(F32)
    d_mix_high, d_mix_low = split_float(jnp.sum(side_sum, axis=1, keepdims=True))
    side_own = jnp.where(
        mine_high, d_mix_high, jnp.where(mine_low, d_mix_low, jnp.zeros((), BF16))
    )
    d_back = exchange(jnp.concatenate([d_sum, side_own], axis=1))
    y_send = pair_sum(jnp.dot(inner_act, down_mat, preferred_element_type=F32) * row_mix)
    d_y = (d_rows.astype(F32) * row_mix).astype(BF16)
    grad_gate = jnp.einsum("rd,rf->df", rows, d_gate, preferred_element_type=F32)[None]
    grad_up = jnp.einsum("rd,rf->df", rows, d_up, preferred_element_type=F32)[None]
    grad_down = jnp.einsum("rf,rd->fd", inner_act, d_y, preferred_element_type=F32)[None]

    d_out = cotangent.astype(F32) * valid_float
    d_token = jnp.dot(token_table, d_back, preferred_element_type=F32)
    d_mix = d_token[:, D : D + experts] + d_token[:, D + experts : D + 2 * experts]
    d_logits = (mix * (d_mix - jnp.sum(mix * d_mix, axis=1, keepdims=True))).astype(BF16)
    grad_router_part = jnp.einsum("td,te->de", normed_two, d_logits, preferred_element_type=F32)
    d_normed_two = d_token[:, :D] + jnp.einsum(
        "te,de->td", d_logits, router, preferred_element_type=F32
    )
    gain_moe_part = lax.dot_general(
        d_normed_two * hidden_one,
        scale_two,
        (((0,), (0,)), ((), ())),
        precision=lax.Precision.HIGHEST,
        preferred_element_type=F32,
    )
    extras = jnp.pad(
        jnp.concatenate([grad_router_part, gain_moe_part], axis=1),
        ((0, 0), (QKV, slab - QKV - experts - 1)),
    )
    along_two = gain_two * d_normed_two
    d_hidden = (
        d_out
        + scale_two * along_two
        - hidden_one
        * (
            scale_two
            * scale_two
            * scale_two
            * jnp.mean(along_two * hidden_one, axis=-1, keepdims=True)
        )
    )
    d_proj = d_hidden.astype(BF16)
    d_attn = jnp.einsum(
        "td,id->ti", d_proj, full_out[:, :D], preferred_element_type=F32
    ).astype(BF16)
    d_attn_rows = lax.all_to_all(d_attn, TEAM, split_axis=1, concat_axis=0, tiled=True)
    d_attn_rows, y_send = lax.optimization_barrier((d_attn_rows, y_send))
    y_back = exchange(y_send)
    d_query, d_kv_all = attend_back(
        lengths, meta, query, d_attn_rows, attn_rows, lse, kv_all
    )
    d_proj, y_back = lax.optimization_barrier((d_proj, y_back))
    d_proj_group = lax.all_gather(d_proj, TEAM, axis=0, tiled=True)
    out_part = jnp.einsum(
        "ti,td->id", attn_rows, d_proj_group, preferred_element_type=F32
    ).astype(BF16)
    grad_out = lax.psum_scatter(out_part, "tg", scatter_dimension=0, tiled=True).astype(F32)
    d_kv_all, y_back = lax.optimization_barrier((d_kv_all, y_back))
    output = (
        valid_float * (hidden_one + jnp.dot(token_table, y_back, preferred_element_type=F32))
    ).astype(BF16)
    d_kv_parts = lax.all_to_all(
        d_kv_all.reshape(planes, rows_group, KV), "tg", split_axis=0, concat_axis=0, tiled=True
    )
    head = lax.axis_index("head")
    turns = jnp.stack([heads - 1 - head, head]).astype(jnp.int32)
    d_qkv, theirs = merge_back(turns[:1], d_query, d_kv_parts, own_slab, heads)
    theirs = lax.ppermute(theirs, "head", partner)
    ours = slab_back(turns[1:], d_qkv, own_slab, heads)
    grad_in = (
        jnp.einsum("td,ti->di", normed_one, d_qkv, preferred_element_type=F32) + extras
    ).astype(BF16)
    grad_in = grad_in.reshape(in_group, planes, rows_dev, slab).transpose(1, 0, 2, 3)
    grad_planes = lax.all_to_all(grad_in, "tg", split_axis=0, concat_axis=0, tiled=True)
    grad_sum = jnp.sum(grad_planes.astype(F32), axis=0).astype(BF16)
    grad_parts = lax.all_to_all(grad_sum, TEAM, split_axis=0, concat_axis=0, tiled=True)
    ours = (ours.astype(F32) + theirs.astype(F32)).astype(BF16)
    d_normed_one = line_sum(ours.reshape(members, tok_dev, D), member)
    (
        grad_query,
        grad_key,
        grad_value,
        grad_router,
        grad_gain_attn,
        grad_gain_moe,
    ) = finish_grads(grad_parts, by_group, experts)
    scale_one = rms_scale(own_x)
    along_one = gain_one * d_normed_one
    input_grad = (
        d_hidden
        + scale_one * along_one
        - own_x
        * (
            scale_one
            * scale_one
            * scale_one
            * jnp.mean(along_one * own_x, axis=-1, keepdims=True)
        )
    ).astype(BF16)
    return (
        output,
        input_grad,
        grad_query,
        grad_key,
        grad_value,
        grad_out,
        grad_router,
        grad_gain_attn,
        grad_gain_moe,
        grad_gate,
        grad_up,
        grad_down,
    )


def solution(mesh):
    heads = mesh.shape["head"]
    members = HK // heads
    planes = mesh.shape["blk"] // members
    inner = Mesh(mesh.devices.reshape(heads, members, planes), ALL)
    rows = P(ALL, None)
    placed = (
        rows,
        P(),
        rows,
        rows,
        rows,
        rows,
        rows,
        rows,
        P(ALL),
        P(ALL),
        P(BLK, None, "head"),
        P(BLK, None, "head"),
        P(BLK, "head", None),
        rows,
    )
    return jax.shard_map(
        shards,
        mesh=inner,
        in_specs=placed,
        out_specs=(
            rows,
            rows,
            rows,
            rows,
            rows,
            rows,
            rows,
            P(ALL),
            P(ALL),
            P(BLK, None, "head"),
            P(BLK, None, "head"),
            P(BLK, "head", None),
        ),
        check_vma=False,
    )
```

```python
import functools
import math

import jax
import jax.numpy as jnp
from jax import lax
from jax.experimental import pallas as pl
from jax.experimental.pallas import tpu as pltpu
from jax.sharding import Mesh
from jax.sharding import PartitionSpec as P


D = 1536
HQ = 24
HK = 8
HD = 64
GROUP = HQ // HK
QW = GROUP * HD
KV = 2 * HD
QKV = QW + KV
LANE = 128
EPS = 1e-05
NEG = -1e30
BQ = 128
KEYS = 256
WIDTHS = (3, 1)
WIDTHS_BACK = (2, 1)
F32 = jnp.float32
BF16 = jnp.bfloat16

TEAM = ("head", "hg")
BLK = ("hg", "tg")
ALL = ("head", "hg", "tg")


def pad_up(count):
    return -(-count // LANE) * LANE


def rms_scale(values):
    return lax.rsqrt(jnp.mean(values * values, axis=-1, keepdims=True) + EPS)


def doc_ranges(lengths_ref, segments, q_pos, first):
    start = jnp.zeros_like(q_pos)
    low = jnp.int32(0)
    end = jnp.int32(0)
    for j in range(segments):
        end = end + lengths_ref[j]
        start = jnp.where(q_pos >= end, end, start)
        low = jnp.where(first >= end, end, low)
    return start, low // KEYS


def head_rows(rows, h, shift):
    part = rows[:, h * HD : (h + 1) * HD]
    zero = jnp.zeros_like(part)
    return jnp.concatenate([zero, part] if shift else [part, zero], axis=1)


def dot_nt(a, b):
    return lax.dot_general(a, b, (((1,), (1,)), ((), ())), preferred_element_type=F32)


def dot_tn(a, b):
    return lax.dot_general(a, b, (((0,), (0,)), ((), ())), preferred_element_type=F32)


def key_place(block, parts, planes):
    first = block * parts
    return [((first + t) % planes, (first + t) // planes) for t in range(parts)]


def allowed_keys(block, start, q_pos):
    k_pos = block * KEYS + lax.broadcasted_iota(jnp.int32, (KEYS, BQ), 0)
    mask = (k_pos >= start) & (k_pos <= q_pos)
    return jnp.concatenate([mask] * GROUP, axis=1)


def in_widths(widths, low, high, visit, state):
    base = low
    for width in widths:
        turns = (high - base) // width
        state = lax.fori_loop(0, turns, functools.partial(visit, width, base), state)
        base = base + turns * width
    return state


def place_pieces(meta_ref, pieces, kv_ref):
    planes = len(pieces)
    for distance, piece in enumerate(pieces):
        kv_ref[(meta_ref[0] + planes - distance) % planes] = piece[...]


def attend_kernel(lengths_ref, meta_ref, q_ref, *refs, segments):
    pieces, (o_ref, lse_ref, kv_ref) = refs[:-3], refs[-3:]
    planes = kv_ref.shape[0]
    place_pieces(meta_ref, pieces, kv_ref)

    def one(step, carry):
        first = (step * planes + meta_ref[0]) * BQ
        rows = pl.ds(pl.multiple_of(step * BQ, BQ), BQ)
        q_pos = first + lax.broadcasted_iota(jnp.int32, (1, BQ), 1)
        start, low = doc_ranges(lengths_ref, segments, q_pos, first)
        high = (first + BQ - 1) // KEYS + 1
        q_part = q_ref[rows, :]
        queries = jnp.concatenate([head_rows(q_part, h, False) for h in range(GROUP)], axis=0)
        queries = queries * jnp.asarray(HD**-0.5, BF16)

        def visit(width, base, turn, state):
            run_max, run_sum, acc = state
            parts = []
            scores = []
            for u in range(width):
                block = base + turn * width + u
                places = key_place(block, KEYS // BQ, planes)
                part = jnp.concatenate([kv_ref[p, r] for p, r in places], axis=0)
                mask = allowed_keys(block, start, q_pos)
                parts.append(part[:, HD:])
                scores.append(jnp.where(mask, dot_nt(part, queries), NEG))
            new_max = run_max
            for value in scores:
                new_max = jnp.maximum(new_max, jnp.max(value, axis=0, keepdims=True))
            shrink = jnp.exp(run_max - new_max)
            run_sum = run_sum * shrink
            acc = acc * shrink
            for part, value in zip(parts, scores):
                weights = jnp.exp(value - new_max)
                run_sum = run_sum + jnp.sum(weights, axis=0, keepdims=True)
                acc = acc + dot_tn(part, weights.astype(BF16))
            return new_max, run_sum, acc

        begin = (
            jnp.full((1, GROUP * BQ), NEG, F32),
            jnp.zeros((1, GROUP * BQ), F32),
            jnp.zeros((HD, GROUP * BQ), F32),
        )
        top, total, acc = in_widths(WIDTHS, low, high, visit, begin)
        out = acc / total
        o_ref[rows, :] = jnp.concatenate(
            [out[:, h * BQ : (h + 1) * BQ] for h in range(GROUP)], axis=0
        ).T.astype(BF16)
        lse_ref[step] = top + jnp.log(total)
        return carry

    lax.fori_loop(0, q_ref.shape[0] // BQ, one, 0)


def attend_back_kernel(
    lengths_ref,
    meta_ref,
    q_ref,
    do_ref,
    o_ref,
    lse_ref,
    *refs,
    segments,
):
    planes = (len(refs) - 3) // 2
    pieces, dq_ref, sends = refs[:planes], refs[planes], refs[planes + 1 : 2 * planes + 1]
    kv_ref, acc_ref = refs[-2:]
    place_pieces(meta_ref, pieces, kv_ref)
    scale = HD**-0.5
    acc_ref[...] = jnp.zeros_like(acc_ref)

    def one(step, carry):
        first = (step * planes + meta_ref[0]) * BQ
        rows = pl.ds(pl.multiple_of(step * BQ, BQ), BQ)
        q_pos = first + lax.broadcasted_iota(jnp.int32, (1, BQ), 1)
        start, low = doc_ranges(lengths_ref, segments, q_pos, first)
        high = (first + BQ - 1) // KEYS + 1
        q_part = q_ref[rows, :]
        do_part = do_ref[rows, :]
        queries = jnp.concatenate([head_rows(q_part, h, False) for h in range(GROUP)], axis=0)
        queries = queries * jnp.asarray(scale, BF16)
        d_outs = jnp.concatenate([head_rows(do_part, h, True) for h in range(GROUP)], axis=0)
        products = (do_part.astype(F32) * o_ref[rows, :].astype(F32)).T
        row_dots = jnp.concatenate(
            [
                jnp.sum(products[h * HD : (h + 1) * HD], axis=0, keepdims=True)
                for h in range(GROUP)
            ],
            axis=1,
        )
        both = jnp.concatenate([queries, d_outs], axis=0)
        lse = lse_ref[step]

        def visit(width, base, turn, d_query):
            total = []
            for u in range(width):
                block = base + turn * width + u
                places = key_place(block, KEYS // BQ, planes)
                part = jnp.concatenate([kv_ref[p, r] for p, r in places], axis=0)
                mask = allowed_keys(block, start, q_pos)
                probs = jnp.where(mask, jnp.exp(dot_nt(part, queries) - lse), 0.0)
                d_scores = (probs * (dot_nt(part, d_outs) - row_dots)).astype(BF16)
                value = jnp.dot(
                    jnp.concatenate([d_scores, probs.astype(BF16)], axis=1),
                    both,
                    preferred_element_type=F32,
                )
                total.append((places, value))
                d_query = d_query + dot_tn(part[:, :HD], d_scores)
            for places, value in total:
                for t, (p, r) in enumerate(places):
                    acc_ref[p, r] += value[t * BQ : (t + 1) * BQ]
            return d_query

        begin = jnp.zeros((HD, GROUP * BQ), F32)
        d_query = in_widths(WIDTHS_BACK, low, high, visit, begin) * scale
        dq_ref[rows, :] = jnp.concatenate(
            [d_query[:, h * BQ : (h + 1) * BQ] for h in range(GROUP)], axis=0
        ).T.astype(BF16)
        return carry

    lax.fori_loop(0, q_ref.shape[0] // BQ, one, 0)
    for distance, send in enumerate(sends):
        send[...] = acc_ref[(meta_ref[0] + distance) % planes].astype(BF16)


def vmem_specs(count):
    return [pl.BlockSpec(memory_space=pltpu.SMEM)] * 2 + [
        pl.BlockSpec(memory_space=pltpu.VMEM)
    ] * count


def attend(lengths, meta, query, pieces):
    rows = query.shape[0]
    whole = (len(pieces),) + pieces[0].shape
    return pl.pallas_call(
        functools.partial(attend_kernel, segments=lengths.shape[0]),
        out_shape=(
            jax.ShapeDtypeStruct((rows, QW), BF16),
            jax.ShapeDtypeStruct((rows // BQ, 1, GROUP * BQ), F32),
        ),
        in_specs=vmem_specs(1 + len(pieces)),
        scratch_shapes=[pltpu.VMEM(whole, BF16)],
        compiler_params=pltpu.CompilerParams(
            vmem_limit_bytes=math.prod(whole) * 6 + (10 << 20)
        ),
        name="attend",
    )(lengths, meta, query, *pieces)


def attend_back(lengths, meta, query, d_out, out, lse, pieces):
    rows = query.shape[0]
    whole = (len(pieces),) + pieces[0].shape
    send = jax.ShapeDtypeStruct(pieces[0].shape, BF16)
    return pl.pallas_call(
        functools.partial(attend_back_kernel, segments=lengths.shape[0]),
        out_shape=(jax.ShapeDtypeStruct((rows, QW), BF16),) + (send,) * len(pieces),
        in_specs=vmem_specs(4 + len(pieces)),
        scratch_shapes=[pltpu.VMEM(whole, BF16), pltpu.VMEM(whole, F32)],
        compiler_params=pltpu.CompilerParams(
            vmem_limit_bytes=math.prod(whole) * 14 + (10 << 20)
        ),
        name="attend_back",
    )(lengths, meta, query, d_out, out, lse, *pieces)


def project_kernel(place_ref, *refs, members):
    pieces = refs[: 2 * (2 * members - 1)]
    slab_ref, normed_ref, q_ref, kv_ref, weight_ref, gain_ref, x_ref, sems = refs[len(pieces) :]
    planes, team, rows, _ = slab_ref.shape
    member, head = place_ref[0], place_ref[1]
    copies = []
    for side in range(2):
        for shift in range(1 - members, members):
            index = len(copies)
            block = member + shift
            fits = (block >= 0) & (block < members)
            row = jnp.clip(jnp.abs(side - head) * members + block, 0, team - 1) * BQ
            copy = pltpu.make_async_copy(
                pieces[index], x_ref.at[pl.ds(pl.multiple_of(row, BQ), BQ), :], sems.at[index]
            )
            copies.append((fits, copy))
    for fits, copy in copies:
        pl.when(fits)(copy.start)
    for g in range(team):
        for p in range(planes):
            at = (g * planes + p) * rows
            weight_ref[at : at + rows, :] = slab_ref[p, g]
    low = QKV // LANE * LANE
    side = weight_ref[:, low : low + LANE].astype(F32).T
    gain_ref[...] = side[QKV - low : QKV - low + 1]
    for fits, copy in copies:
        pl.when(fits)(copy.wait)

    def one(step, carry):
        block = chunk_of(step, BQ)
        x = x_ref[block, :].astype(F32)
        normed = (x * rms_scale(x) * gain_ref[...]).astype(BF16)
        normed_ref[block, :] = normed
        qkv = jnp.dot(normed, weight_ref[...], preferred_element_type=F32).astype(BF16)
        q_ref[block, :] = qkv[:, :QW]
        kv_ref[block, :] = qkv[:, QW:QKV]
        return carry

    lax.fori_loop(0, x_ref.shape[0] // BQ, one, 0)


def project(place, pieces, slab, members):
    planes, team, _, width = slab.shape
    rows = team * BQ
    return pl.pallas_call(
        functools.partial(project_kernel, members=members),
        out_shape=(
            jax.ShapeDtypeStruct((rows, D), BF16),
            jax.ShapeDtypeStruct((rows, QW), BF16),
            jax.ShapeDtypeStruct((rows, KV), BF16),
            jax.ShapeDtypeStruct((D, width), BF16),
            jax.ShapeDtypeStruct((1, D), F32),
        ),
        in_specs=[pl.BlockSpec(memory_space=pltpu.SMEM)]
        + [pl.BlockSpec(memory_space=pltpu.HBM)] * len(pieces)
        + [pl.BlockSpec(memory_space=pltpu.VMEM)],
        scratch_shapes=[
            pltpu.VMEM((rows, D), BF16),
            pltpu.SemaphoreType.DMA((len(pieces),)),
        ],
        compiler_params=pltpu.CompilerParams(vmem_limit_bytes=planes * rows * KV * 4 + (16 << 20)),
        name="project",
    )(place, *pieces, slab)


def line_gather(rows, members, partner):
    own = {0: rows}
    other = {}
    up = down = rows
    other[0] = lax.ppermute(rows, "head", partner)
    last = members - 1
    for turn in range(last):
        up = lax.ppermute(up, "hg", [(m, m + 1) for m in range(turn, last)])
        down = lax.ppermute(down, "hg", [(m, m - 1) for m in range(last - turn, 0, -1)])
        up, down = lax.optimization_barrier((up, down))
        own[-1 - turn], own[1 + turn] = up, down
        other[-1 - turn] = lax.ppermute(up, "head", partner)
        other[1 + turn] = lax.ppermute(down, "head", partner)
    order = range(-last, members)
    return [own[k] for k in order] + [other[k] for k in order]


def chunk_of(index, width):
    return pl.ds(pl.multiple_of(index * width, width), width)


def grad_in_kernel(normed_ref, qkv_ref, extras_ref, out_ref):
    planes, _, rows, width = out_ref.shape
    step = D // 4
    owners = step // rows
    low = width - extras_ref.shape[1]

    def one(index, carry):
        part = chunk_of(index, step)
        value = dot_tn(normed_ref[:, part], qkv_ref[...])
        value = jnp.concatenate([value[:, :low], value[:, low:] + extras_ref[part, :]], axis=1)
        value = value.astype(BF16)
        for k in range(owners):
            owner = index * owners + k
            out_ref[owner % planes, owner // planes] = value[k * rows : (k + 1) * rows]
        return carry

    lax.fori_loop(0, D // step, one, 0)


def grad_in_parts(normed, d_qkv, extras, planes, team):
    rows = D // (planes * team)
    width = d_qkv.shape[1]
    return pl.pallas_call(
        grad_in_kernel,
        out_shape=jax.ShapeDtypeStruct((planes, team, rows, width), BF16),
        compiler_params=pltpu.CompilerParams(vmem_limit_bytes=16 << 20),
        name="grad_in",
    )(normed, d_qkv, extras)


def attn_back_kernel(proj_ref, full_ref, out_ref):
    step = 3 * LANE

    def one(index, carry):
        part = chunk_of(index, step)
        out_ref[:, part] = dot_nt(proj_ref[...], full_ref[part, :D]).astype(BF16)
        return carry

    lax.fori_loop(0, D // step, one, 0)


def attn_back(d_proj, full_out):
    return pl.pallas_call(
        attn_back_kernel,
        out_shape=jax.ShapeDtypeStruct(d_proj.shape, BF16),
        compiler_params=pltpu.CompilerParams(vmem_limit_bytes=10 << 20),
        name="attn_back",
    )(d_proj, full_out)


def side_columns(shape, expert, experts):
    column = lax.broadcasted_iota(jnp.int32, shape, 1)
    return column == expert, column == expert + experts


def expert_kernel(
    expert_ref,
    x_own_ref,
    x_other_ref,
    d_own_ref,
    d_other_ref,
    gate_ref,
    up_ref,
    down_ref,
    back_ref,
    inner_ref,
    d_gate_ref,
    d_up_ref,
    x_ref,
    d_ref,
    sems,
    *,
    experts,
):
    slots = x_own_ref.shape[0]
    pairs = (
        (x_own_ref, x_ref.at[:slots]),
        (x_other_ref, x_ref.at[slots:]),
        (d_own_ref, d_ref.at[:slots]),
        (d_other_ref, d_ref.at[slots:]),
    )
    copies = [
        pltpu.make_async_copy(source, target, sems.at[index])
        for index, (source, target) in enumerate(pairs)
    ]
    for copy in copies:
        copy.start()
    for copy in copies:
        copy.wait()
    half = gate_ref.shape[1] // 2

    def rows_of(turn, carry):
        block = chunk_of(turn, slots)
        side = x_ref[block, D:].astype(F32)
        high, low = side_columns(side.shape, expert_ref[0], experts)
        mix = jnp.sum(jnp.where(high | low, side, 0.0), axis=1, keepdims=True)

        def units_of(index, d_mix):
            part = chunk_of(index, half)
            x = x_ref[block, :D]
            gate = jnp.dot(x, gate_ref[:, part], preferred_element_type=F32)
            up = jnp.dot(x, up_ref[:, part], preferred_element_type=F32)
            d_inner = dot_nt(d_ref[block, :], down_ref[part, :])
            sigmoid = jax.nn.sigmoid(gate)
            act = gate * sigmoid
            inner = act * up
            d_mix = d_mix + jnp.sum(d_inner * inner, axis=1, keepdims=True)
            d_inner = d_inner * mix
            inner_ref[block, part] = (inner * mix).astype(BF16)
            d_gate_ref[block, part] = (
                d_inner * up * sigmoid * (1.0 + gate * (1.0 - sigmoid))
            ).astype(BF16)
            d_up_ref[block, part] = (d_inner * act).astype(BF16)
            return d_mix

        d_mix = lax.fori_loop(0, 2, units_of, jnp.zeros((slots, 1), F32))

        def columns_of(index, carry):
            part = chunk_of(index, D // 3)
            back_ref[block, part] = (
                dot_nt(d_gate_ref[block, :], gate_ref[part, :])
                + dot_nt(d_up_ref[block, :], up_ref[part, :])
            ).astype(BF16)
            return carry

        lax.fori_loop(0, 3, columns_of, 0)
        d_high, d_low = split_float(d_mix)
        back_ref[block, D:] = jnp.where(
            high, d_high.astype(F32), jnp.where(low, d_low.astype(F32), 0.0)
        ).astype(BF16)
        return carry

    lax.fori_loop(0, 2, rows_of, 0)


def visit_expert(expert, x_own, x_other, d_own, d_other, gate, up, down, experts):
    slots, width = x_own.shape
    inner = jax.ShapeDtypeStruct((2 * slots, gate.shape[1]), BF16)
    return pl.pallas_call(
        functools.partial(expert_kernel, experts=experts),
        out_shape=(jax.ShapeDtypeStruct((2 * slots, width), BF16), inner, inner, inner),
        in_specs=[pl.BlockSpec(memory_space=pltpu.SMEM)]
        + [pl.BlockSpec(memory_space=pl.ANY)] * 4
        + [pl.BlockSpec(memory_space=pltpu.VMEM)] * 3,
        scratch_shapes=[
            pltpu.VMEM((2 * slots, width), BF16),
            pltpu.VMEM((2 * slots, D), BF16),
            pltpu.SemaphoreType.DMA((4,)),
        ],
        compiler_params=pltpu.CompilerParams(vmem_limit_bytes=26 << 20),
        name="expert",
    )(expert, x_own, x_other, d_own, d_other, gate, up, down)


def pair_kernel(expert_ref, own_ref, other_ref, out_ref, *, experts):
    total = own_ref[...].astype(F32) + other_ref[...].astype(F32)
    out_ref[:, :D] = total[:, :D].astype(BF16)
    side = total[:, D:]
    d_high, d_low = split_float(jnp.sum(side, axis=1, keepdims=True))
    high, low = side_columns(side.shape, expert_ref[0], experts)
    out_ref[:, D:] = jnp.where(
        high, d_high.astype(F32), jnp.where(low, d_low.astype(F32), 0.0)
    ).astype(BF16)


def pair_back(expert, partial, theirs, experts):
    slots, width = theirs.shape
    step = slots // 4
    return pl.pallas_call(
        functools.partial(pair_kernel, experts=experts),
        grid=(slots // step,),
        out_shape=jax.ShapeDtypeStruct((slots, width), BF16),
        in_specs=[
            pl.BlockSpec(memory_space=pltpu.SMEM),
            pl.BlockSpec((step, width), lambda i: (i, 0)),
            pl.BlockSpec((step, width), lambda i: (i, 0)),
        ],
        out_specs=pl.BlockSpec((step, width), lambda i: (i, 0)),
        compiler_params=pltpu.CompilerParams(vmem_limit_bytes=8 << 20),
        name="pair_back",
    )(expert, partial, theirs)


def expert_grads_kernel(
    x_own_ref,
    x_other_ref,
    d_own_ref,
    d_other_ref,
    inner_ref,
    d_gate_ref,
    d_up_ref,
    gate_ref,
    up_ref,
    down_ref,
):
    x = jnp.concatenate([x_own_ref[...], x_other_ref[...]], axis=0)
    d = jnp.concatenate([d_own_ref[...], d_other_ref[...]], axis=0)
    gate_ref[0] = dot_tn(x, d_gate_ref[...])
    up_ref[0] = dot_tn(x, d_up_ref[...])
    down_ref[0] = dot_tn(inner_ref[...], d)


def expert_grads(x_own, x_other, d_own, d_other, inner, d_gate, d_up):
    slots = x_own.shape[0]
    width = inner.shape[1]
    step = LANE
    part = pl.BlockSpec((slots, step), lambda i: (0, i))
    whole = pl.BlockSpec(inner.shape, lambda i: (0, 0))
    return pl.pallas_call(
        expert_grads_kernel,
        grid=(D // step,),
        out_shape=(
            jax.ShapeDtypeStruct((1, D, width), F32),
            jax.ShapeDtypeStruct((1, D, width), F32),
            jax.ShapeDtypeStruct((1, width, D), F32),
        ),
        in_specs=[part] * 4 + [whole] * 3,
        out_specs=[
            pl.BlockSpec((1, step, width), lambda i: (0, i, 0)),
            pl.BlockSpec((1, step, width), lambda i: (0, i, 0)),
            pl.BlockSpec((1, width, step), lambda i: (0, 0, i)),
        ],
        compiler_params=pltpu.CompilerParams(vmem_limit_bytes=24 << 20),
        name="expert_grads",
    )(x_own, x_other, d_own, d_other, inner, d_gate, d_up)


def row_of(weights, values):
    return lax.dot_general(
        weights,
        values,
        (((1,), (1,)), ((), ())),
        precision=lax.Precision.HIGHEST,
        preferred_element_type=F32,
    )[:1]


def finish_kernel(parts_ref, slab_ref, q_ref, k_ref, v_ref, router_ref, attn_ref, moe_ref):
    rows, experts = router_ref.shape
    width = slab_ref.shape[2] - QKV

    def two_groups(index, carry):
        small, along = carry
        parts = [parts_ref[2 * index + k].astype(F32) for k in range(2)]
        q_ref[:, chunk_of(index, 2 * QW)] = jnp.concatenate([p[:, :QW] for p in parts], axis=1)
        for ref, at in ((k_ref, QW), (v_ref, QW + HD)):
            ref[:, chunk_of(index, 2 * HD)] = jnp.concatenate(
                [p[:, at : at + HD] for p in parts], axis=1
            )
        for k, part in enumerate(parts):
            along = along + part[:, :QKV] * slab_ref[2 * index + k, :, :QKV].astype(F32)
            small = small + part[:, QKV:]
        return small, along

    begin = (jnp.zeros((rows, width), F32), jnp.zeros((rows, QKV), F32))
    small, along = lax.fori_loop(0, HK // 2, two_groups, begin)
    router_ref[...] = small[:, :experts]
    column = lax.broadcasted_iota(jnp.int32, (8, width), 1)
    moe_ref[...] = row_of((column == experts).astype(F32), small)
    gain = row_of((column == 0).astype(F32), slab_ref[0, :, QKV:].astype(F32))
    attn_ref[...] = row_of(jnp.ones((8, QKV), F32), along) / gain


def finish_grads(parts, by_group, experts):
    rows = by_group.shape[1]

    def shape(columns):
        return jax.ShapeDtypeStruct((rows, columns), F32)

    line = jax.ShapeDtypeStruct((1, rows), F32)
    out = pl.pallas_call(
        finish_kernel,
        out_shape=(
            shape(HQ * HD),
            shape(HK * HD),
            shape(HK * HD),
            shape(experts),
            line,
            line,
        ),
        compiler_params=pltpu.CompilerParams(vmem_limit_bytes=8 << 20),
        name="finish_grads",
    )(parts, by_group)
    return out[:4] + (out[4].reshape(rows), out[5].reshape(rows))


def slab_rows(qkv_ref, slab_ref, out_ref, turn):
    def one(index, carry):
        source = chunk_of(turn * (out_ref.shape[0] // (2 * BQ)) + index, 2 * BQ)
        out_ref[chunk_of(index, 2 * BQ), :] = dot_nt(qkv_ref[source, :], slab_ref[...]).astype(BF16)
        return carry

    lax.fori_loop(0, out_ref.shape[0] // (2 * BQ), one, 0)


def merge_kernel(turn_ref, dq_ref, *refs):
    parts, (slab_ref, qkv_ref, out_ref) = refs[:-3], refs[-3:]
    zero = jnp.zeros((2 * BQ, qkv_ref.shape[1] - QKV), BF16)

    def one(index, carry):
        rows = chunk_of(index, 2 * BQ)
        d_kv = sum(part[rows, :].astype(F32) for part in parts).astype(BF16)
        qkv_ref[rows, :] = jnp.concatenate([dq_ref[rows, :], d_kv, zero], axis=1)
        return carry

    lax.fori_loop(0, dq_ref.shape[0] // (2 * BQ), one, 0)
    slab_rows(qkv_ref, slab_ref, out_ref, turn_ref[0])


def merge_back(turn, d_query, d_kv_parts, slab, heads):
    rows = d_query.shape[0]
    planes = len(d_kv_parts)
    return pl.pallas_call(
        merge_kernel,
        out_shape=(
            jax.ShapeDtypeStruct((rows, slab.shape[1]), BF16),
            jax.ShapeDtypeStruct((rows // heads, D), BF16),
        ),
        in_specs=[pl.BlockSpec(memory_space=pltpu.SMEM)]
        + [pl.BlockSpec(memory_space=pltpu.VMEM)] * (planes + 2),
        compiler_params=pltpu.CompilerParams(vmem_limit_bytes=planes * rows * KV * 4 + (12 << 20)),
        name="merge_back",
    )(turn, d_query, *d_kv_parts, slab)


def slab_back_kernel(turn_ref, qkv_ref, slab_ref, out_ref):
    slab_rows(qkv_ref, slab_ref, out_ref, turn_ref[0])


def slab_back(turn, d_qkv, slab, heads):
    return pl.pallas_call(
        slab_back_kernel,
        out_shape=jax.ShapeDtypeStruct((d_qkv.shape[0] // heads, D), BF16),
        in_specs=[
            pl.BlockSpec(memory_space=pltpu.SMEM),
            pl.BlockSpec(memory_space=pltpu.VMEM),
            pl.BlockSpec(memory_space=pltpu.VMEM),
        ],
        compiler_params=pltpu.CompilerParams(vmem_limit_bytes=10 << 20),
        name="slab_back",
    )(turn, d_qkv, slab)


def line_sum(parts, place):
    last = parts.shape[0] - 1
    up = jnp.zeros(parts.shape[1:], BF16)
    down = jnp.zeros(parts.shape[1:], BF16)

    def block(index):
        return lax.dynamic_index_in_dim(parts, jnp.clip(index, 0, last), 0, keepdims=False)

    for turn in range(last):
        to_up = block(place + last - turn)
        to_down = block(place - last + turn)
        if turn:
            to_up = (to_up.astype(F32) + up.astype(F32)).astype(BF16)
            to_down = (to_down.astype(F32) + down.astype(F32)).astype(BF16)
        up = lax.ppermute(to_up, "hg", [(m, m + 1) for m in range(turn + 1)])
        down = lax.ppermute(to_down, "hg", [(m, m - 1) for m in range(last, last - turn - 1, -1)])
        up, down = lax.optimization_barrier((up, down))
    return block(place).astype(F32) + up.astype(F32) + down.astype(F32)


def split_float(value):
    high = value.astype(BF16)
    return high, (value - high.astype(F32)).astype(BF16)


def shards(
    tokens,
    lengths,
    expert_ids,
    w_query,
    w_key,
    w_value,
    w_out,
    w_router,
    gain_attn,
    gain_moe,
    w_gate,
    w_up,
    w_down,
    cotangent,
):
    heads = lax.axis_size("head")
    planes = lax.axis_size("tg")
    members = lax.axis_size("hg")
    blk_count = planes * members
    in_group = heads * members
    tok_dev = tokens.shape[0]
    rows_dev = w_query.shape[0]
    experts = blk_count
    capacity = max(2, 3 * tok_dev // experts)
    slots = experts * capacity
    rows_group = in_group * tok_dev
    slab = pad_up(QKV + experts + 1)
    plane = lax.axis_index("tg")
    member = lax.axis_index("hg")
    blk_index = member * planes + plane
    partner = [(i, heads - 1 - i) for i in range(heads)]

    by_group = jnp.concatenate(
        [
            w_query.reshape(rows_dev, in_group, QW),
            w_key.reshape(rows_dev, in_group, HD),
            w_value.reshape(rows_dev, in_group, HD),
            jnp.broadcast_to(gain_attn[:, None, None], (rows_dev, in_group, 1)),
            jnp.zeros((rows_dev, in_group, slab - QKV - 1), BF16),
        ],
        axis=2,
    ).transpose(1, 0, 2)
    slab_team = lax.all_to_all(
        by_group, TEAM, split_axis=0, concat_axis=0, tiled=True
    )
    own_slab = lax.all_to_all(
        jnp.broadcast_to(slab_team[None], (planes, in_group, rows_dev, slab)),
        "tg",
        split_axis=0,
        concat_axis=0,
        tiled=True,
    )
    pieces = line_gather(tokens, members, partner)
    out_shard = jnp.concatenate(
        [
            w_out,
            w_router,
            gain_moe[:, None],
            jnp.zeros((rows_dev, pad_up(experts + 1) - experts - 1), BF16),
        ],
        axis=1,
    )
    full_out = lax.all_gather(out_shard, ALL, axis=0, tiled=True)

    seq_ends = jnp.cumsum(lengths)
    own_pos = (lax.axis_index("head") * blk_count + blk_index) * tok_dev + jnp.arange(
        tok_dev, dtype=jnp.int32
    )
    valid_bool = own_pos < seq_ends[-2]
    valid_float = valid_bool.astype(F32)[:, None]
    expert_range = jnp.arange(experts, dtype=jnp.int32)
    pair_experts = expert_ids.reshape(-1)
    live_pairs = jnp.repeat(valid_bool, 2)
    onehot = (
        (pair_experts[:, None] == expert_range[None, :]) & live_pairs[:, None]
    ).astype(jnp.int32)
    earlier = jnp.cumsum(onehot, axis=0) - onehot
    slot_index = jnp.sum(earlier * onehot, axis=1)
    kept_pairs = live_pairs & (slot_index < capacity)
    flat_index = jnp.where(kept_pairs, pair_experts * capacity + slot_index, -1)
    slot_ids = jnp.arange(slots, dtype=jnp.int32)
    token_index = flat_index.reshape(tok_dev, 2)
    token_table = (
        (token_index[:, 0][:, None] == slot_ids[None, :])
        | (token_index[:, 1][:, None] == slot_ids[None, :])
    ).astype(BF16)
    picked = (expert_ids[:, 0][:, None] == expert_range[None, :]) | (
        expert_ids[:, 1][:, None] == expert_range[None, :]
    )
    side = pad_up(2 * experts)
    side_zeros = jnp.zeros((tok_dev, side - 2 * experts), BF16)

    def exchange(rows):
        return lax.all_to_all(
            rows.reshape(experts, capacity, rows.shape[1]),
            BLK,
            split_axis=0,
            concat_axis=0,
            tiled=True,
        ).reshape(slots, rows.shape[1])

    def pick_rows(values):
        return lax.dot_general(
            token_table, values, (((0,), (0,)), ((), ())), preferred_element_type=F32
        ).astype(BF16)

    normed_one, query, kv_own, own_slab, gain_one = project(
        jnp.stack([member, lax.axis_index("head")]).astype(jnp.int32),
        pieces,
        own_slab,
        members,
    )

    def next_planes(distance):
        return [(p, (p + distance) % planes) for p in range(planes)]

    kv_own = kv_own.reshape(in_group, tok_dev, KV)
    kv_pieces = [kv_own] + [
        lax.ppermute(kv_own, "tg", next_planes(distance)) for distance in range(1, planes)
    ]
    d_send = pick_rows(cotangent)
    d_sent = exchange(d_send)
    meta = plane.astype(jnp.int32).reshape(1)
    attn_rows, lse = attend(lengths, meta, query, kv_pieces)
    d_sent, attn_rows = lax.optimization_barrier((d_sent, attn_rows))
    attn_tokens = lax.all_to_all(attn_rows, TEAM, split_axis=0, concat_axis=1, tiled=True)

    own_x = tokens.astype(F32)
    hidden_one = own_x + jnp.dot(attn_tokens, full_out[:, :D], preferred_element_type=F32)
    scale_two = rms_scale(hidden_one)
    gain_two = full_out[:, D + experts].astype(F32)[None, :]
    router = full_out[:, D : D + experts]
    normed_two = (hidden_one * scale_two * gain_two).astype(BF16)
    logits = jnp.dot(normed_two, router, preferred_element_type=F32)
    mix = jax.nn.softmax(jnp.where(picked, logits, NEG), axis=1)
    mix_high, mix_low = split_float(mix)
    moe_send = pick_rows(jnp.concatenate([normed_two, mix_high, mix_low, side_zeros], axis=1))
    moe_sent = exchange(moe_send)
    moe_other = lax.ppermute(moe_sent, "head", partner)
    d_other = lax.ppermute(d_sent, "head", partner)

    down_mat = w_down[0]
    expert = blk_index.astype(jnp.int32).reshape(1)
    partial, inner_mixed, d_gate, d_up = visit_expert(
        expert, moe_sent, moe_other, d_sent, d_other, w_gate[0], w_up[0], down_mat, experts
    )
    summed = pair_back(
        expert, partial, lax.ppermute(partial[slots:], "head", partner), experts
    )
    d_back = exchange(summed)
    y_part = jnp.dot(inner_mixed, down_mat, preferred_element_type=F32)
    y_theirs = lax.ppermute(y_part[slots:].astype(BF16), "head", partner)
    y_send = (y_part[:slots] + y_theirs.astype(F32)).astype(BF16)
    grad_gate, grad_up, grad_down = expert_grads(
        moe_sent, moe_other, d_sent, d_other, inner_mixed, d_gate, d_up
    )

    d_out = cotangent.astype(F32) * valid_float
    d_token = jnp.dot(token_table, d_back, preferred_element_type=F32)
    d_mix = d_token[:, D : D + experts] + d_token[:, D + experts : D + 2 * experts]
    d_logits = (mix * (d_mix - jnp.sum(mix * d_mix, axis=1, keepdims=True))).astype(BF16)
    grad_router_part = jnp.einsum("td,te->de", normed_two, d_logits, preferred_element_type=F32)
    d_normed_two = d_token[:, :D] + jnp.einsum(
        "te,de->td", d_logits, router, preferred_element_type=F32
    )
    gain_moe_part = lax.dot_general(
        d_normed_two * hidden_one,
        scale_two,
        (((0,), (0,)), ((), ())),
        precision=lax.Precision.HIGHEST,
        preferred_element_type=F32,
    )
    extras = jnp.pad(
        jnp.concatenate([grad_router_part, gain_moe_part], axis=1),
        ((0, 0), (QKV % LANE, slab - QKV - experts - 1)),
    )
    along_two = gain_two * d_normed_two
    d_hidden = (
        d_out
        + scale_two * along_two
        - hidden_one
        * (
            scale_two
            * scale_two
            * scale_two
            * jnp.mean(along_two * hidden_one, axis=-1, keepdims=True)
        )
    )
    d_proj = d_hidden.astype(BF16)
    d_attn = attn_back(d_proj, full_out)
    d_attn_rows = lax.all_to_all(d_attn, TEAM, split_axis=1, concat_axis=0, tiled=True)
    d_attn_rows, y_send = lax.optimization_barrier((d_attn_rows, y_send))
    y_back = exchange(y_send)
    d_query, *d_kv_sends = attend_back(lengths, meta, query, d_attn_rows, attn_rows, lse, kv_pieces)
    d_proj, d_query = lax.optimization_barrier((d_proj, d_query))
    d_proj_group = lax.all_gather(d_proj, TEAM, axis=0, tiled=True)
    out_part = jnp.einsum(
        "ti,td->id", attn_rows, d_proj_group, preferred_element_type=F32
    ).astype(BF16)
    grad_out = lax.psum_scatter(out_part, "tg", scatter_dimension=0, tiled=True).astype(F32)
    d_kv_parts = [d_kv_sends[0]] + [
        lax.ppermute(d_kv_sends[distance], "tg", next_planes(distance))
        for distance in range(1, planes)
    ]
    d_kv_parts = [part.reshape(rows_group, KV) for part in d_kv_parts]
    head = lax.axis_index("head")
    turns = jnp.stack([heads - 1 - head, head]).astype(jnp.int32)
    d_qkv, theirs = merge_back(turns[:1], d_query, d_kv_parts, own_slab, heads)
    theirs = lax.ppermute(theirs, "head", partner)
    ours = slab_back(turns[1:], d_qkv, own_slab, heads)
    d_qkv, y_back = lax.optimization_barrier((d_qkv, y_back))
    output = (
        valid_float * (hidden_one + jnp.dot(token_table, y_back, preferred_element_type=F32))
    ).astype(BF16)
    grad_in = grad_in_parts(normed_one, d_qkv, extras, planes, in_group)
    grad_planes = lax.all_to_all(grad_in, "tg", split_axis=0, concat_axis=0, tiled=True)
    grad_sum = jnp.sum(grad_planes.astype(F32), axis=0).astype(BF16)
    grad_parts = lax.all_to_all(grad_sum, TEAM, split_axis=0, concat_axis=0, tiled=True)
    ours = (ours.astype(F32) + theirs.astype(F32)).astype(BF16)
    d_normed_one = line_sum(ours.reshape(members, tok_dev, D), member)
    (
        grad_query,
        grad_key,
        grad_value,
        grad_router,
        grad_gain_attn,
        grad_gain_moe,
    ) = finish_grads(grad_parts, by_group, experts)
    scale_one = rms_scale(own_x)
    along_one = gain_one * d_normed_one
    input_grad = (
        d_hidden
        + scale_one * along_one
        - own_x
        * (
            scale_one
            * scale_one
            * scale_one
            * jnp.mean(along_one * own_x, axis=-1, keepdims=True)
        )
    ).astype(BF16)
    return (
        output,
        input_grad,
        grad_query,
        grad_key,
        grad_value,
        grad_out,
        grad_router,
        grad_gain_attn,
        grad_gain_moe,
        grad_gate,
        grad_up,
        grad_down,
    )


def solution(mesh):
    heads = mesh.shape["head"]
    members = HK // heads
    planes = mesh.shape["blk"] // members
    inner = Mesh(mesh.devices.reshape(heads, members, planes), ALL)
    rows = P(ALL, None)
    placed = (
        rows,
        P(),
        rows,
        rows,
        rows,
        rows,
        rows,
        rows,
        P(ALL),
        P(ALL),
        P(BLK, None, "head"),
        P(BLK, None, "head"),
        P(BLK, "head", None),
        rows,
    )
    return jax.shard_map(
        shards,
        mesh=inner,
        in_specs=placed,
        out_specs=(
            rows,
            rows,
            rows,
            rows,
            rows,
            rows,
            rows,
            P(ALL),
            P(ALL),
            P(BLK, None, "head"),
            P(BLK, None, "head"),
            P(BLK, "head", None),
        ),
        check_vma=False,
    )
```

```python
import functools
import math

import jax
import jax.numpy as jnp
from jax import lax
from jax.experimental import pallas as pl
from jax.experimental.pallas import tpu as pltpu
from jax.sharding import Mesh
from jax.sharding import PartitionSpec as P


D = 1536
HQ = 24
HK = 8
HD = 64
GROUP = HQ // HK
QW = GROUP * HD
KV = 2 * HD
QKV = QW + KV
LANE = 128
EPS = 1e-05
NEG = -1e30
BQ = 128
KEYS = 256
WIDTHS = (3, 1)
WIDTHS_BACK = (2, 1)
F32 = jnp.float32
BF16 = jnp.bfloat16

TEAM = ("head", "hg")
BLK = ("hg", "tg")
ALL = ("head", "hg", "tg")


def pad_up(count):
    return -(-count // LANE) * LANE


def rms_scale(values):
    return lax.rsqrt(jnp.mean(values * values, axis=-1, keepdims=True) + EPS)


def doc_ranges(lengths_ref, segments, q_pos, first):
    start = jnp.zeros_like(q_pos)
    low = jnp.int32(0)
    end = jnp.int32(0)
    for j in range(segments):
        end = end + lengths_ref[j]
        start = jnp.where(q_pos >= end, end, start)
        low = jnp.where(first >= end, end, low)
    return start, low // KEYS


def head_rows(rows, h, shift):
    part = rows[:, h * HD : (h + 1) * HD]
    zero = jnp.zeros_like(part)
    return jnp.concatenate([zero, part] if shift else [part, zero], axis=1)


def dot_nt(a, b):
    return lax.dot_general(a, b, (((1,), (1,)), ((), ())), preferred_element_type=F32)


def dot_tn(a, b):
    return lax.dot_general(a, b, (((0,), (0,)), ((), ())), preferred_element_type=F32)


def key_place(block, parts, planes):
    first = block * parts
    return [((first + t) % planes, (first + t) // planes) for t in range(parts)]


def allowed_keys(block, start, q_pos):
    k_pos = block * KEYS + lax.broadcasted_iota(jnp.int32, (KEYS, BQ), 0)
    mask = (k_pos >= start) & (k_pos <= q_pos)
    return jnp.concatenate([mask] * GROUP, axis=1)


def in_widths(widths, low, high, visit, state):
    base = low
    for width in widths:
        turns = (high - base) // width
        state = lax.fori_loop(0, turns, functools.partial(visit, width, base), state)
        base = base + turns * width
    return state


def place_pieces(meta_ref, pieces, kv_ref):
    planes = len(pieces)
    for distance, piece in enumerate(pieces):
        kv_ref[(meta_ref[0] + planes - distance) % planes] = piece[...]


def attend_kernel(lengths_ref, meta_ref, q_ref, *refs, segments):
    pieces, (o_ref, lse_ref, kv_ref) = refs[:-3], refs[-3:]
    planes = kv_ref.shape[0]
    place_pieces(meta_ref, pieces, kv_ref)

    def one(step, carry):
        first = (step * planes + meta_ref[0]) * BQ
        rows = pl.ds(pl.multiple_of(step * BQ, BQ), BQ)
        q_pos = first + lax.broadcasted_iota(jnp.int32, (1, BQ), 1)
        start, low = doc_ranges(lengths_ref, segments, q_pos, first)
        high = (first + BQ - 1) // KEYS + 1
        q_part = q_ref[rows, :]
        queries = jnp.concatenate([head_rows(q_part, h, False) for h in range(GROUP)], axis=0)
        queries = queries * jnp.asarray(HD**-0.5, BF16)

        def visit(width, base, turn, state):
            run_max, run_sum, acc = state
            parts = []
            scores = []
            for u in range(width):
                block = base + turn * width + u
                places = key_place(block, KEYS // BQ, planes)
                part = jnp.concatenate([kv_ref[p, r] for p, r in places], axis=0)
                mask = allowed_keys(block, start, q_pos)
                parts.append(part[:, HD:])
                scores.append(jnp.where(mask, dot_nt(part, queries), NEG))
            new_max = run_max
            for value in scores:
                new_max = jnp.maximum(new_max, jnp.max(value, axis=0, keepdims=True))
            shrink = jnp.exp(run_max - new_max)
            run_sum = run_sum * shrink
            acc = acc * shrink
            for part, value in zip(parts, scores):
                weights = jnp.exp(value - new_max)
                run_sum = run_sum + jnp.sum(weights, axis=0, keepdims=True)
                acc = acc + dot_tn(part, weights.astype(BF16))
            return new_max, run_sum, acc

        begin = (
            jnp.full((1, GROUP * BQ), NEG, F32),
            jnp.zeros((1, GROUP * BQ), F32),
            jnp.zeros((HD, GROUP * BQ), F32),
        )
        top, total, acc = in_widths(WIDTHS, low, high, visit, begin)
        out = acc / total
        o_ref[rows, :] = jnp.concatenate(
            [out[:, h * BQ : (h + 1) * BQ] for h in range(GROUP)], axis=0
        ).T.astype(BF16)
        lse_ref[step] = top + jnp.log(total)
        return carry

    lax.fori_loop(0, q_ref.shape[0] // BQ, one, 0)


def attend_back_kernel(
    lengths_ref,
    meta_ref,
    q_ref,
    do_ref,
    o_ref,
    lse_ref,
    *refs,
    segments,
):
    planes = (len(refs) - 3) // 2
    pieces, dq_ref, sends = refs[:planes], refs[planes], refs[planes + 1 : 2 * planes + 1]
    kv_ref, acc_ref = refs[-2:]
    place_pieces(meta_ref, pieces, kv_ref)
    scale = HD**-0.5
    acc_ref[...] = jnp.zeros_like(acc_ref)

    def one(step, carry):
        first = (step * planes + meta_ref[0]) * BQ
        rows = pl.ds(pl.multiple_of(step * BQ, BQ), BQ)
        q_pos = first + lax.broadcasted_iota(jnp.int32, (1, BQ), 1)
        start, low = doc_ranges(lengths_ref, segments, q_pos, first)
        high = (first + BQ - 1) // KEYS + 1
        q_part = q_ref[rows, :]
        do_part = do_ref[rows, :]
        queries = jnp.concatenate([head_rows(q_part, h, False) for h in range(GROUP)], axis=0)
        queries = queries * jnp.asarray(scale, BF16)
        d_outs = jnp.concatenate([head_rows(do_part, h, True) for h in range(GROUP)], axis=0)
        products = (do_part.astype(F32) * o_ref[rows, :].astype(F32)).T
        row_dots = jnp.concatenate(
            [
                jnp.sum(products[h * HD : (h + 1) * HD], axis=0, keepdims=True)
                for h in range(GROUP)
            ],
            axis=1,
        )
        both = jnp.concatenate([queries, d_outs], axis=0)
        lse = lse_ref[step]

        def visit(width, base, turn, d_query):
            total = []
            for u in range(width):
                block = base + turn * width + u
                places = key_place(block, KEYS // BQ, planes)
                part = jnp.concatenate([kv_ref[p, r] for p, r in places], axis=0)
                mask = allowed_keys(block, start, q_pos)
                probs = jnp.where(mask, jnp.exp(dot_nt(part, queries) - lse), 0.0)
                d_scores = (probs * (dot_nt(part, d_outs) - row_dots)).astype(BF16)
                value = jnp.dot(
                    jnp.concatenate([d_scores, probs.astype(BF16)], axis=1),
                    both,
                    preferred_element_type=F32,
                )
                total.append((places, value))
                d_query = d_query + dot_tn(part[:, :HD], d_scores)
            for places, value in total:
                for t, (p, r) in enumerate(places):
                    acc_ref[p, r] += value[t * BQ : (t + 1) * BQ]
            return d_query

        begin = jnp.zeros((HD, GROUP * BQ), F32)
        d_query = in_widths(WIDTHS_BACK, low, high, visit, begin) * scale
        dq_ref[rows, :] = jnp.concatenate(
            [d_query[:, h * BQ : (h + 1) * BQ] for h in range(GROUP)], axis=0
        ).T.astype(BF16)
        return carry

    lax.fori_loop(0, q_ref.shape[0] // BQ, one, 0)
    for distance, send in enumerate(sends):
        send[...] = acc_ref[(meta_ref[0] + distance) % planes].astype(BF16)


def vmem_specs(count):
    return [pl.BlockSpec(memory_space=pltpu.SMEM)] * 2 + [
        pl.BlockSpec(memory_space=pltpu.VMEM)
    ] * count


def attend(lengths, meta, query, pieces):
    rows = query.shape[0]
    whole = (len(pieces),) + pieces[0].shape
    return pl.pallas_call(
        functools.partial(attend_kernel, segments=lengths.shape[0]),
        out_shape=(
            jax.ShapeDtypeStruct((rows, QW), BF16),
            jax.ShapeDtypeStruct((rows // BQ, 1, GROUP * BQ), F32),
        ),
        in_specs=vmem_specs(1 + len(pieces)),
        scratch_shapes=[pltpu.VMEM(whole, BF16)],
        compiler_params=pltpu.CompilerParams(
            vmem_limit_bytes=math.prod(whole) * 6 + (10 << 20)
        ),
    )(lengths, meta, query, *pieces)


def attend_back(lengths, meta, query, d_out, out, lse, pieces):
    rows = query.shape[0]
    whole = (len(pieces),) + pieces[0].shape
    send = jax.ShapeDtypeStruct(pieces[0].shape, BF16)
    return pl.pallas_call(
        functools.partial(attend_back_kernel, segments=lengths.shape[0]),
        out_shape=(jax.ShapeDtypeStruct((rows, QW), BF16),) + (send,) * len(pieces),
        in_specs=vmem_specs(4 + len(pieces)),
        scratch_shapes=[pltpu.VMEM(whole, BF16), pltpu.VMEM(whole, F32)],
        compiler_params=pltpu.CompilerParams(
            vmem_limit_bytes=math.prod(whole) * 14 + (10 << 20)
        ),
    )(lengths, meta, query, d_out, out, lse, *pieces)


def project_kernel(place_ref, *refs, members):
    pieces = refs[: 2 * (2 * members - 1)]
    slab_ref, normed_ref, q_ref, kv_ref, weight_ref, gain_ref, x_ref, sems = refs[len(pieces) :]
    planes, team, rows, _ = slab_ref.shape
    member, head = place_ref[0], place_ref[1]
    copies = []
    for side in range(2):
        for shift in range(1 - members, members):
            index = len(copies)
            block = member + shift
            fits = (block >= 0) & (block < members)
            row = jnp.clip(jnp.abs(side - head) * members + block, 0, team - 1) * BQ
            copy = pltpu.make_async_copy(
                pieces[index], x_ref.at[pl.ds(pl.multiple_of(row, BQ), BQ), :], sems.at[index]
            )
            copies.append((fits, copy))
    for fits, copy in copies:
        pl.when(fits)(copy.start)
    for g in range(team):
        for p in range(planes):
            at = (g * planes + p) * rows
            weight_ref[at : at + rows, :] = slab_ref[p, g]
    low = QKV // LANE * LANE
    side = weight_ref[:, low : low + LANE].astype(F32).T
    gain_ref[...] = side[QKV - low : QKV - low + 1]
    for fits, copy in copies:
        pl.when(fits)(copy.wait)

    def one(step, carry):
        block = chunk_of(step, BQ)
        x = x_ref[block, :].astype(F32)
        normed = (x * rms_scale(x) * gain_ref[...]).astype(BF16)
        normed_ref[block, :] = normed
        qkv = jnp.dot(normed, weight_ref[...], preferred_element_type=F32).astype(BF16)
        q_ref[block, :] = qkv[:, :QW]
        kv_ref[block, :] = qkv[:, QW:QKV]
        return carry

    lax.fori_loop(0, x_ref.shape[0] // BQ, one, 0)


def project(place, pieces, slab, members):
    planes, team, _, width = slab.shape
    rows = team * BQ
    return pl.pallas_call(
        functools.partial(project_kernel, members=members),
        out_shape=(
            jax.ShapeDtypeStruct((rows, D), BF16),
            jax.ShapeDtypeStruct((rows, QW), BF16),
            jax.ShapeDtypeStruct((rows, KV), BF16),
            jax.ShapeDtypeStruct((D, width), BF16),
            jax.ShapeDtypeStruct((1, D), F32),
        ),
        in_specs=[pl.BlockSpec(memory_space=pltpu.SMEM)]
        + [pl.BlockSpec(memory_space=pltpu.HBM)] * len(pieces)
        + [pl.BlockSpec(memory_space=pltpu.VMEM)],
        scratch_shapes=[
            pltpu.VMEM((rows, D), BF16),
            pltpu.SemaphoreType.DMA((len(pieces),)),
        ],
        compiler_params=pltpu.CompilerParams(vmem_limit_bytes=planes * rows * KV * 4 + (16 << 20)),
    )(place, *pieces, slab)


def line_gather(rows, members, partner):
    own = {0: rows}
    other = {}
    up = down = rows
    other[0] = lax.ppermute(rows, "head", partner)
    last = members - 1
    for turn in range(last):
        up = lax.ppermute(up, "hg", [(m, m + 1) for m in range(turn, last)])
        down = lax.ppermute(down, "hg", [(m, m - 1) for m in range(last - turn, 0, -1)])
        up, down = lax.optimization_barrier((up, down))
        own[-1 - turn], own[1 + turn] = up, down
        other[-1 - turn] = lax.ppermute(up, "head", partner)
        other[1 + turn] = lax.ppermute(down, "head", partner)
    order = range(-last, members)
    return [own[k] for k in order] + [other[k] for k in order]


def chunk_of(index, width):
    return pl.ds(pl.multiple_of(index * width, width), width)


def grad_in_kernel(normed_ref, qkv_ref, extras_ref, out_ref):
    planes, _, rows, width = out_ref.shape
    step = D // 4
    owners = step // rows
    low = width - extras_ref.shape[1]

    def one(index, carry):
        part = chunk_of(index, step)
        value = dot_tn(normed_ref[:, part], qkv_ref[...])
        value = jnp.concatenate([value[:, :low], value[:, low:] + extras_ref[part, :]], axis=1)
        value = value.astype(BF16)
        for k in range(owners):
            owner = index * owners + k
            out_ref[owner % planes, owner // planes] = value[k * rows : (k + 1) * rows]
        return carry

    lax.fori_loop(0, D // step, one, 0)


def grad_in_parts(normed, d_qkv, extras, planes, team):
    rows = D // (planes * team)
    width = d_qkv.shape[1]
    return pl.pallas_call(
        grad_in_kernel,
        out_shape=jax.ShapeDtypeStruct((planes, team, rows, width), BF16),
        compiler_params=pltpu.CompilerParams(vmem_limit_bytes=16 << 20),
    )(normed, d_qkv, extras)


def attn_back_kernel(proj_ref, full_ref, out_ref):
    step = 3 * LANE

    def one(index, carry):
        part = chunk_of(index, step)
        out_ref[:, part] = dot_nt(proj_ref[...], full_ref[part, :D]).astype(BF16)
        return carry

    lax.fori_loop(0, D // step, one, 0)


def attn_back(d_proj, full_out):
    return pl.pallas_call(
        attn_back_kernel,
        out_shape=jax.ShapeDtypeStruct(d_proj.shape, BF16),
        compiler_params=pltpu.CompilerParams(vmem_limit_bytes=10 << 20),
    )(d_proj, full_out)


def side_columns(shape, expert, experts):
    column = lax.broadcasted_iota(jnp.int32, shape, 1)
    return column == expert, column == expert + experts


def expert_kernel(
    expert_ref,
    x_own_ref,
    x_other_ref,
    d_own_ref,
    d_other_ref,
    gate_ref,
    up_ref,
    down_ref,
    back_ref,
    inner_ref,
    d_gate_ref,
    d_up_ref,
    x_ref,
    d_ref,
    sems,
    *,
    experts,
):
    slots = x_own_ref.shape[0]
    pairs = (
        (x_own_ref, x_ref.at[:slots]),
        (x_other_ref, x_ref.at[slots:]),
        (d_own_ref, d_ref.at[:slots]),
        (d_other_ref, d_ref.at[slots:]),
    )
    copies = [
        pltpu.make_async_copy(source, target, sems.at[index])
        for index, (source, target) in enumerate(pairs)
    ]
    for copy in copies:
        copy.start()
    for copy in copies:
        copy.wait()
    half = gate_ref.shape[1] // 2

    def rows_of(turn, carry):
        block = chunk_of(turn, slots)
        side = x_ref[block, D:].astype(F32)
        high, low = side_columns(side.shape, expert_ref[0], experts)
        mix = jnp.sum(jnp.where(high | low, side, 0.0), axis=1, keepdims=True)

        def units_of(index, d_mix):
            part = chunk_of(index, half)
            x = x_ref[block, :D]
            gate = jnp.dot(x, gate_ref[:, part], preferred_element_type=F32)
            up = jnp.dot(x, up_ref[:, part], preferred_element_type=F32)
            d_inner = dot_nt(d_ref[block, :], down_ref[part, :])
            sigmoid = jax.nn.sigmoid(gate)
            act = gate * sigmoid
            inner = act * up
            d_mix = d_mix + jnp.sum(d_inner * inner, axis=1, keepdims=True)
            d_inner = d_inner * mix
            inner_ref[block, part] = (inner * mix).astype(BF16)
            d_gate_ref[block, part] = (
                d_inner * up * sigmoid * (1.0 + gate * (1.0 - sigmoid))
            ).astype(BF16)
            d_up_ref[block, part] = (d_inner * act).astype(BF16)
            return d_mix

        d_mix = lax.fori_loop(0, 2, units_of, jnp.zeros((slots, 1), F32))

        def columns_of(index, carry):
            part = chunk_of(index, D // 3)
            back_ref[block, part] = (
                dot_nt(d_gate_ref[block, :], gate_ref[part, :])
                + dot_nt(d_up_ref[block, :], up_ref[part, :])
            ).astype(BF16)
            return carry

        lax.fori_loop(0, 3, columns_of, 0)
        d_high, d_low = split_float(d_mix)
        back_ref[block, D:] = jnp.where(
            high, d_high.astype(F32), jnp.where(low, d_low.astype(F32), 0.0)
        ).astype(BF16)
        return carry

    lax.fori_loop(0, 2, rows_of, 0)


def visit_expert(expert, x_own, x_other, d_own, d_other, gate, up, down, experts):
    slots, width = x_own.shape
    inner = jax.ShapeDtypeStruct((2 * slots, gate.shape[1]), BF16)
    return pl.pallas_call(
        functools.partial(expert_kernel, experts=experts),
        out_shape=(jax.ShapeDtypeStruct((2 * slots, width), BF16), inner, inner, inner),
        in_specs=[pl.BlockSpec(memory_space=pltpu.SMEM)]
        + [pl.BlockSpec(memory_space=pl.ANY)] * 4
        + [pl.BlockSpec(memory_space=pltpu.VMEM)] * 3,
        scratch_shapes=[
            pltpu.VMEM((2 * slots, width), BF16),
            pltpu.VMEM((2 * slots, D), BF16),
            pltpu.SemaphoreType.DMA((4,)),
        ],
        compiler_params=pltpu.CompilerParams(vmem_limit_bytes=26 << 20),
    )(expert, x_own, x_other, d_own, d_other, gate, up, down)


def pair_kernel(expert_ref, own_ref, other_ref, out_ref, *, experts):
    total = own_ref[...].astype(F32) + other_ref[...].astype(F32)
    out_ref[:, :D] = total[:, :D].astype(BF16)
    side = total[:, D:]
    d_high, d_low = split_float(jnp.sum(side, axis=1, keepdims=True))
    high, low = side_columns(side.shape, expert_ref[0], experts)
    out_ref[:, D:] = jnp.where(
        high, d_high.astype(F32), jnp.where(low, d_low.astype(F32), 0.0)
    ).astype(BF16)


def pair_back(expert, partial, theirs, experts):
    slots, width = theirs.shape
    step = slots // 4
    return pl.pallas_call(
        functools.partial(pair_kernel, experts=experts),
        grid=(slots // step,),
        out_shape=jax.ShapeDtypeStruct((slots, width), BF16),
        in_specs=[
            pl.BlockSpec(memory_space=pltpu.SMEM),
            pl.BlockSpec((step, width), lambda i: (i, 0)),
            pl.BlockSpec((step, width), lambda i: (i, 0)),
        ],
        out_specs=pl.BlockSpec((step, width), lambda i: (i, 0)),
        compiler_params=pltpu.CompilerParams(vmem_limit_bytes=8 << 20),
    )(expert, partial, theirs)


def expert_grads_kernel(
    x_own_ref,
    x_other_ref,
    d_own_ref,
    d_other_ref,
    inner_ref,
    d_gate_ref,
    d_up_ref,
    gate_ref,
    up_ref,
    down_ref,
):
    x = jnp.concatenate([x_own_ref[...], x_other_ref[...]], axis=0)
    d = jnp.concatenate([d_own_ref[...], d_other_ref[...]], axis=0)
    gate_ref[0] = dot_tn(x, d_gate_ref[...])
    up_ref[0] = dot_tn(x, d_up_ref[...])
    down_ref[0] = dot_tn(inner_ref[...], d)


def expert_grads(x_own, x_other, d_own, d_other, inner, d_gate, d_up):
    slots = x_own.shape[0]
    width = inner.shape[1]
    step = LANE
    part = pl.BlockSpec((slots, step), lambda i: (0, i))
    whole = pl.BlockSpec(inner.shape, lambda i: (0, 0))
    return pl.pallas_call(
        expert_grads_kernel,
        grid=(D // step,),
        out_shape=(
            jax.ShapeDtypeStruct((1, D, width), F32),
            jax.ShapeDtypeStruct((1, D, width), F32),
            jax.ShapeDtypeStruct((1, width, D), F32),
        ),
        in_specs=[part] * 4 + [whole] * 3,
        out_specs=[
            pl.BlockSpec((1, step, width), lambda i: (0, i, 0)),
            pl.BlockSpec((1, step, width), lambda i: (0, i, 0)),
            pl.BlockSpec((1, width, step), lambda i: (0, 0, i)),
        ],
        compiler_params=pltpu.CompilerParams(vmem_limit_bytes=24 << 20),
    )(x_own, x_other, d_own, d_other, inner, d_gate, d_up)


def row_of(weights, values):
    return lax.dot_general(
        weights,
        values,
        (((1,), (1,)), ((), ())),
        precision=lax.Precision.HIGHEST,
        preferred_element_type=F32,
    )[:1]


def finish_kernel(parts_ref, slab_ref, q_ref, k_ref, v_ref, router_ref, attn_ref, moe_ref):
    rows, experts = router_ref.shape
    width = slab_ref.shape[2] - QKV

    def two_groups(index, carry):
        small, along = carry
        parts = [parts_ref[2 * index + k].astype(F32) for k in range(2)]
        q_ref[:, chunk_of(index, 2 * QW)] = jnp.concatenate([p[:, :QW] for p in parts], axis=1)
        for ref, at in ((k_ref, QW), (v_ref, QW + HD)):
            ref[:, chunk_of(index, 2 * HD)] = jnp.concatenate(
                [p[:, at : at + HD] for p in parts], axis=1
            )
        for k, part in enumerate(parts):
            along = along + part[:, :QKV] * slab_ref[2 * index + k, :, :QKV].astype(F32)
            small = small + part[:, QKV:]
        return small, along

    begin = (jnp.zeros((rows, width), F32), jnp.zeros((rows, QKV), F32))
    small, along = lax.fori_loop(0, HK // 2, two_groups, begin)
    router_ref[...] = small[:, :experts]
    column = lax.broadcasted_iota(jnp.int32, (8, width), 1)
    moe_ref[...] = row_of((column == experts).astype(F32), small)
    gain = row_of((column == 0).astype(F32), slab_ref[0, :, QKV:].astype(F32))
    attn_ref[...] = row_of(jnp.ones((8, QKV), F32), along) / gain


def finish_grads(parts, by_group, experts):
    rows = by_group.shape[1]

    def shape(columns):
        return jax.ShapeDtypeStruct((rows, columns), F32)

    line = jax.ShapeDtypeStruct((1, rows), F32)
    out = pl.pallas_call(
        finish_kernel,
        out_shape=(
            shape(HQ * HD),
            shape(HK * HD),
            shape(HK * HD),
            shape(experts),
            line,
            line,
        ),
        compiler_params=pltpu.CompilerParams(vmem_limit_bytes=8 << 20),
    )(parts, by_group)
    return out[:4] + (out[4].reshape(rows), out[5].reshape(rows))


def slab_rows(qkv_ref, slab_ref, out_ref, turn):
    def one(index, carry):
        source = chunk_of(turn * (out_ref.shape[0] // (2 * BQ)) + index, 2 * BQ)
        out_ref[chunk_of(index, 2 * BQ), :] = dot_nt(qkv_ref[source, :], slab_ref[...]).astype(BF16)
        return carry

    lax.fori_loop(0, out_ref.shape[0] // (2 * BQ), one, 0)


def merge_kernel(turn_ref, dq_ref, *refs):
    parts, (slab_ref, qkv_ref, out_ref) = refs[:-3], refs[-3:]
    zero = jnp.zeros((2 * BQ, qkv_ref.shape[1] - QKV), BF16)

    def one(index, carry):
        rows = chunk_of(index, 2 * BQ)
        d_kv = sum(part[rows, :].astype(F32) for part in parts).astype(BF16)
        qkv_ref[rows, :] = jnp.concatenate([dq_ref[rows, :], d_kv, zero], axis=1)
        return carry

    lax.fori_loop(0, dq_ref.shape[0] // (2 * BQ), one, 0)
    slab_rows(qkv_ref, slab_ref, out_ref, turn_ref[0])


def merge_back(turn, d_query, d_kv_parts, slab, heads):
    rows = d_query.shape[0]
    planes = len(d_kv_parts)
    return pl.pallas_call(
        merge_kernel,
        out_shape=(
            jax.ShapeDtypeStruct((rows, slab.shape[1]), BF16),
            jax.ShapeDtypeStruct((rows // heads, D), BF16),
        ),
        in_specs=[pl.BlockSpec(memory_space=pltpu.SMEM)]
        + [pl.BlockSpec(memory_space=pltpu.VMEM)] * (planes + 2),
        compiler_params=pltpu.CompilerParams(vmem_limit_bytes=planes * rows * KV * 4 + (12 << 20)),
    )(turn, d_query, *d_kv_parts, slab)


def slab_back_kernel(turn_ref, qkv_ref, slab_ref, out_ref):
    slab_rows(qkv_ref, slab_ref, out_ref, turn_ref[0])


def slab_back(turn, d_qkv, slab, heads):
    return pl.pallas_call(
        slab_back_kernel,
        out_shape=jax.ShapeDtypeStruct((d_qkv.shape[0] // heads, D), BF16),
        in_specs=[
            pl.BlockSpec(memory_space=pltpu.SMEM),
            pl.BlockSpec(memory_space=pltpu.VMEM),
            pl.BlockSpec(memory_space=pltpu.VMEM),
        ],
        compiler_params=pltpu.CompilerParams(vmem_limit_bytes=10 << 20),
    )(turn, d_qkv, slab)


def line_sum(parts, place):
    last = parts.shape[0] - 1
    up = jnp.zeros(parts.shape[1:], BF16)
    down = jnp.zeros(parts.shape[1:], BF16)

    def block(index):
        return lax.dynamic_index_in_dim(parts, jnp.clip(index, 0, last), 0, keepdims=False)

    for turn in range(last):
        to_up = block(place + last - turn)
        to_down = block(place - last + turn)
        if turn:
            to_up = (to_up.astype(F32) + up.astype(F32)).astype(BF16)
            to_down = (to_down.astype(F32) + down.astype(F32)).astype(BF16)
        up = lax.ppermute(to_up, "hg", [(m, m + 1) for m in range(turn + 1)])
        down = lax.ppermute(to_down, "hg", [(m, m - 1) for m in range(last, last - turn - 1, -1)])
        up, down = lax.optimization_barrier((up, down))
    return block(place).astype(F32) + up.astype(F32) + down.astype(F32)


def split_float(value):
    high = value.astype(BF16)
    return high, (value - high.astype(F32)).astype(BF16)


def shards(
    tokens,
    lengths,
    expert_ids,
    w_query,
    w_key,
    w_value,
    w_out,
    w_router,
    gain_attn,
    gain_moe,
    w_gate,
    w_up,
    w_down,
    cotangent,
):
    heads = lax.axis_size("head")
    planes = lax.axis_size("tg")
    members = lax.axis_size("hg")
    blk_count = planes * members
    in_group = heads * members
    tok_dev = tokens.shape[0]
    rows_dev = w_query.shape[0]
    experts = blk_count
    capacity = max(2, 3 * tok_dev // experts)
    slots = experts * capacity
    rows_group = in_group * tok_dev
    slab = pad_up(QKV + experts + 1)
    plane = lax.axis_index("tg")
    member = lax.axis_index("hg")
    blk_index = member * planes + plane
    partner = [(i, heads - 1 - i) for i in range(heads)]

    by_group = jnp.concatenate(
        [
            w_query.reshape(rows_dev, in_group, QW),
            w_key.reshape(rows_dev, in_group, HD),
            w_value.reshape(rows_dev, in_group, HD),
            jnp.broadcast_to(gain_attn[:, None, None], (rows_dev, in_group, 1)),
            jnp.zeros((rows_dev, in_group, slab - QKV - 1), BF16),
        ],
        axis=2,
    ).transpose(1, 0, 2)
    slab_team = lax.all_to_all(
        by_group, TEAM, split_axis=0, concat_axis=0, tiled=True
    )
    own_slab = lax.all_to_all(
        jnp.broadcast_to(slab_team[None], (planes, in_group, rows_dev, slab)),
        "tg",
        split_axis=0,
        concat_axis=0,
        tiled=True,
    )
    pieces = line_gather(tokens, members, partner)
    out_shard = jnp.concatenate(
        [
            w_out,
            w_router,
            gain_moe[:, None],
            jnp.zeros((rows_dev, pad_up(experts + 1) - experts - 1), BF16),
        ],
        axis=1,
    )
    full_out = lax.all_gather(out_shard, ALL, axis=0, tiled=True)

    seq_ends = jnp.cumsum(lengths)
    own_pos = (lax.axis_index("head") * blk_count + blk_index) * tok_dev + jnp.arange(
        tok_dev, dtype=jnp.int32
    )
    valid_bool = own_pos < seq_ends[-2]
    valid_float = valid_bool.astype(F32)[:, None]
    expert_range = jnp.arange(experts, dtype=jnp.int32)
    pair_experts = expert_ids.reshape(-1)
    live_pairs = jnp.repeat(valid_bool, 2)
    onehot = (
        (pair_experts[:, None] == expert_range[None, :]) & live_pairs[:, None]
    ).astype(jnp.int32)
    earlier = jnp.cumsum(onehot, axis=0) - onehot
    slot_index = jnp.sum(earlier * onehot, axis=1)
    kept_pairs = live_pairs & (slot_index < capacity)
    flat_index = jnp.where(kept_pairs, pair_experts * capacity + slot_index, -1)
    slot_ids = jnp.arange(slots, dtype=jnp.int32)
    token_index = flat_index.reshape(tok_dev, 2)
    token_table = (
        (token_index[:, 0][:, None] == slot_ids[None, :])
        | (token_index[:, 1][:, None] == slot_ids[None, :])
    ).astype(BF16)
    picked = (expert_ids[:, 0][:, None] == expert_range[None, :]) | (
        expert_ids[:, 1][:, None] == expert_range[None, :]
    )
    side = pad_up(2 * experts)
    side_zeros = jnp.zeros((tok_dev, side - 2 * experts), BF16)

    def exchange(rows):
        return lax.all_to_all(
            rows.reshape(experts, capacity, rows.shape[1]),
            BLK,
            split_axis=0,
            concat_axis=0,
            tiled=True,
        ).reshape(slots, rows.shape[1])

    def pick_rows(values):
        return lax.dot_general(
            token_table, values, (((0,), (0,)), ((), ())), preferred_element_type=F32
        ).astype(BF16)

    normed_one, query, kv_own, own_slab, gain_one = project(
        jnp.stack([member, lax.axis_index("head")]).astype(jnp.int32),
        pieces,
        own_slab,
        members,
    )

    def next_planes(distance):
        return [(p, (p + distance) % planes) for p in range(planes)]

    kv_own = kv_own.reshape(in_group, tok_dev, KV)
    kv_pieces = [kv_own] + [
        lax.ppermute(kv_own, "tg", next_planes(distance)) for distance in range(1, planes)
    ]
    d_send = pick_rows(cotangent)
    d_sent = exchange(d_send)
    meta = plane.astype(jnp.int32).reshape(1)
    attn_rows, lse = attend(lengths, meta, query, kv_pieces)
    d_sent, attn_rows = lax.optimization_barrier((d_sent, attn_rows))
    attn_tokens = lax.all_to_all(attn_rows, TEAM, split_axis=0, concat_axis=1, tiled=True)

    own_x = tokens.astype(F32)
    hidden_one = own_x + jnp.dot(attn_tokens, full_out[:, :D], preferred_element_type=F32)
    scale_two = rms_scale(hidden_one)
    gain_two = full_out[:, D + experts].astype(F32)[None, :]
    router = full_out[:, D : D + experts]
    normed_two = (hidden_one * scale_two * gain_two).astype(BF16)
    logits = jnp.dot(normed_two, router, preferred_element_type=F32)
    mix = jax.nn.softmax(jnp.where(picked, logits, NEG), axis=1)
    mix_high, mix_low = split_float(mix)
    moe_send = pick_rows(jnp.concatenate([normed_two, mix_high, mix_low, side_zeros], axis=1))
    moe_sent = exchange(moe_send)
    moe_other = lax.ppermute(moe_sent, "head", partner)
    d_other = lax.ppermute(d_sent, "head", partner)

    down_mat = w_down[0]
    expert = blk_index.astype(jnp.int32).reshape(1)
    partial, inner_mixed, d_gate, d_up = visit_expert(
        expert, moe_sent, moe_other, d_sent, d_other, w_gate[0], w_up[0], down_mat, experts
    )
    summed = pair_back(
        expert, partial, lax.ppermute(partial[slots:], "head", partner), experts
    )
    d_back = exchange(summed)
    y_part = jnp.dot(inner_mixed, down_mat, preferred_element_type=F32)
    y_theirs = lax.ppermute(y_part[slots:].astype(BF16), "head", partner)
    y_send = (y_part[:slots] + y_theirs.astype(F32)).astype(BF16)
    grad_gate, grad_up, grad_down = expert_grads(
        moe_sent, moe_other, d_sent, d_other, inner_mixed, d_gate, d_up
    )

    d_out = cotangent.astype(F32) * valid_float
    d_token = jnp.dot(token_table, d_back, preferred_element_type=F32)
    d_mix = d_token[:, D : D + experts] + d_token[:, D + experts : D + 2 * experts]
    d_logits = (mix * (d_mix - jnp.sum(mix * d_mix, axis=1, keepdims=True))).astype(BF16)
    d_normed_two = d_token[:, :D] + jnp.einsum(
        "te,de->td", d_logits, router, preferred_element_type=F32
    )
    grad_router_part = jnp.einsum("td,te->de", normed_two, d_logits, preferred_element_type=F32)
    gain_moe_part = lax.dot_general(
        d_normed_two * hidden_one,
        scale_two,
        (((0,), (0,)), ((), ())),
        precision=lax.Precision.HIGHEST,
        preferred_element_type=F32,
    )
    extras = jnp.pad(
        jnp.concatenate([grad_router_part, gain_moe_part], axis=1),
        ((0, 0), (QKV % LANE, slab - QKV - experts - 1)),
    )
    along_two = gain_two * d_normed_two
    d_hidden = (
        d_out
        + scale_two * along_two
        - hidden_one
        * (
            scale_two
            * scale_two
            * scale_two
            * jnp.mean(along_two * hidden_one, axis=-1, keepdims=True)
        )
    )
    d_proj = d_hidden.astype(BF16)
    d_attn = attn_back(d_proj, full_out)
    d_attn_rows = lax.all_to_all(d_attn, TEAM, split_axis=1, concat_axis=0, tiled=True)
    d_attn_rows, y_send = lax.optimization_barrier((d_attn_rows, y_send))
    y_back = exchange(y_send)
    d_query, *d_kv_sends = attend_back(lengths, meta, query, d_attn_rows, attn_rows, lse, kv_pieces)
    d_proj, d_query = lax.optimization_barrier((d_proj, d_query))
    d_proj_group = lax.all_gather(d_proj, TEAM, axis=0, tiled=True)
    out_part = jnp.einsum(
        "ti,td->id", attn_rows, d_proj_group, preferred_element_type=F32
    ).astype(BF16)
    grad_out = lax.psum_scatter(out_part, "tg", scatter_dimension=0, tiled=True).astype(F32)
    d_kv_parts = [d_kv_sends[0]]
    for distance in range(1, planes):
        d_kv_parts.append(lax.ppermute(d_kv_sends[distance], "tg", next_planes(distance)))
    d_kv_parts = [part.reshape(rows_group, KV) for part in d_kv_parts]
    head = lax.axis_index("head")
    turns = jnp.stack([heads - 1 - head, head]).astype(jnp.int32)
    d_qkv, theirs = merge_back(turns[:1], d_query, d_kv_parts, own_slab, heads)
    theirs = lax.ppermute(theirs, "head", partner)
    ours = slab_back(turns[1:], d_qkv, own_slab, heads)
    d_qkv, y_back = lax.optimization_barrier((d_qkv, y_back))
    output = (
        valid_float * (hidden_one + jnp.dot(token_table, y_back, preferred_element_type=F32))
    ).astype(BF16)
    grad_in = grad_in_parts(normed_one, d_qkv, extras, planes, in_group)
    grad_planes = lax.all_to_all(grad_in, "tg", split_axis=0, concat_axis=0, tiled=True)
    grad_sum = jnp.sum(grad_planes.astype(F32), axis=0).astype(BF16)
    grad_parts = lax.all_to_all(grad_sum, TEAM, split_axis=0, concat_axis=0, tiled=True)
    ours = (ours.astype(F32) + theirs.astype(F32)).astype(BF16)
    d_normed_one = line_sum(ours.reshape(members, tok_dev, D), member)
    (
        grad_query,
        grad_key,
        grad_value,
        grad_router,
        grad_gain_attn,
        grad_gain_moe,
    ) = finish_grads(grad_parts, by_group, experts)
    scale_one = rms_scale(own_x)
    along_one = gain_one * d_normed_one
    input_grad = (
        d_hidden
        + scale_one * along_one
        - own_x
        * (
            scale_one
            * scale_one
            * scale_one
            * jnp.mean(along_one * own_x, axis=-1, keepdims=True)
        )
    ).astype(BF16)
    return (
        output,
        input_grad,
        grad_query,
        grad_key,
        grad_value,
        grad_out,
        grad_router,
        grad_gain_attn,
        grad_gain_moe,
        grad_gate,
        grad_up,
        grad_down,
    )


def solution(mesh):
    heads = mesh.shape["head"]
    members = HK // heads
    planes = mesh.shape["blk"] // members
    inner = Mesh(mesh.devices.reshape(heads, members, planes), ALL)
    rows = P(ALL, None)
    placed = (
        rows,
        P(),
        rows,
        rows,
        rows,
        rows,
        rows,
        rows,
        P(ALL),
        P(ALL),
        P(BLK, None, "head"),
        P(BLK, None, "head"),
        P(BLK, "head", None),
        rows,
    )
    return jax.shard_map(
        shards,
        mesh=inner,
        in_specs=placed,
        out_specs=(
            rows,
            rows,
            rows,
            rows,
            rows,
            rows,
            rows,
            P(ALL),
            P(ALL),
            P(BLK, None, "head"),
            P(BLK, None, "head"),
            P(BLK, "head", None),
        ),
        check_vma=False,
    )
```
